128 devices in a mesh: rep: 2 (over core), row: 64 (over x, z, y).
Axes of the slice: x: 4, y: 4, z: 4, core: 2. Of those that a mesh axis runs over, the one named last changes fastest.
Arguments:
- tiles: bfloat16 [512, 16, 128, 128], P('row', 'rep'), as said below
- tile_cols: int32 [512, 16], replicated, may hold values from -1 to 511, as said below
Outputs:
- vertex_counts: float32 [512, 128], P('row', 'rep')
The draws below stay inside these ranges and needn't reach their ends.
Inputs may be any that keep to these rules, and one draw needn't show every extreme that they name: `tile_cols`: in each tile row I the filled slots come first and hold distinct tile columns from I - 32 to I, in increasing order; empty slots hold -1. At most 16 slots of a row are filled, and some row has all 16 filled. `tiles`: tiles of empty slots are zero; a tile on the diagonal (column equal to row) is zero on and above its own diagonal.
All inputs are finite; a program needn't handle non-finite values.
Results may differ from the reference program's by a relative error of at most 0.0003.
Values may be sent and summed in bfloat16 or wider, within the bound.
A program may use at most 128 MiB of HBM per device.

```python
import jax
import jax.numpy as jnp
from jax import lax

TILE = 128
TR_DEV = 8
SLOTS = 16
BACK = 4
NTR = 512


def slot_columns(key):
    key = jax.random.fold_in(key, 7)
    reach = BACK * TR_DEV
    rows = jnp.arange(NTR, dtype=jnp.int32)
    lowest = jnp.minimum(1 + SLOTS * rows // NTR, SLOTS)
    filled = jnp.minimum(rows + 1, jax.random.randint(jax.random.fold_in(key, 1), (NTR,), lowest, SLOTS + 1))
    scores = jax.random.randint(jax.random.fold_in(key, 2), (NTR, NTR), 0, 1 << 20)
    colidx = jnp.arange(NTR, dtype=jnp.int32)[None, :]
    inside = (colidx <= rows[:, None]) & (colidx >= rows[:, None] - reach)
    scores = jnp.where(inside, scores, 1 << 21) * NTR + colidx
    order = jnp.argsort(scores, axis=1, stable=True)[:, :SLOTS].astype(jnp.int32)
    slot = jnp.arange(SLOTS, dtype=jnp.int32)
    chosen = jnp.where(slot[None, :] < filled[:, None], order, 2 * NTR)
    chosen = jnp.sort(chosen, axis=1)
    return jnp.where(chosen >= NTR, -1, chosen).astype(jnp.int32)


def draw_tile_cols(key, part):
    return slot_columns(key)


def draw_tiles(key, part):
    cols = slot_columns(key)
    inner = jax.random.fold_in(key, 11)
    shape = (NTR, SLOTS, TILE, TILE)
    values = jax.random.normal(inner, shape, jnp.float32)
    spread = (0.5 * SLOTS * SLOTS * TILE ** 3) ** (-1.0 / 6.0)
    values = spread * (values + 0.1)
    strict = jnp.arange(TILE)[:, None] > jnp.arange(TILE)[None, :]
    diagonal = cols == jnp.arange(NTR, dtype=jnp.int32)[:, None]
    keep = (cols >= 0)[:, :, None, None] & (jnp.logical_not(diagonal)[:, :, None, None] | strict[None, None])
    return jnp.where(keep, values, 0.0).astype(jnp.bfloat16)


def setup_inputs(seed: int = 0) -> dict:
    keys = jax.random.split(jax.random.key(seed), 3)
    tiles = draw_tiles(jax.random.fold_in(keys[2], 71), 0)
    tile_cols = draw_tile_cols(jax.random.fold_in(keys[2], 71), 0)
    return {"tiles": tiles, "tile_cols": tile_cols}


def reference(tiles, tile_cols):
    count_rows = tiles.shape[0]

    def per_row(index):
        cols = tile_cols[index]
        mine = tiles[index].astype(jnp.float32)
        safe = jnp.maximum(cols, 0).astype(jnp.int32)
        panels = tiles[safe].astype(jnp.float32)
        panel_cols = tile_cols[safe]
        match = (panel_cols[:, :, None] == cols[None, None, :]) & (cols >= 0)[None, None, :]
        masks = jnp.einsum("kjp,pac->kjac", match.astype(jnp.float32), mine, precision=lax.Precision.HIGHEST)
        product = jnp.einsum("kab,kjbc->kjac", mine, panels, precision=lax.Precision.HIGHEST)
        return jnp.sum(product * masks, axis=(0, 1, 3))

    return lax.map(per_row, jnp.arange(count_rows, dtype=jnp.int32))
```

```python
import functools

import jax
import jax.numpy as jnp
from jax import lax
from jax.experimental import pallas as pl
from jax.experimental.pallas import tpu as pltpu
from jax.sharding import PartitionSpec as P

MESH = pl.DeviceIdType.MESH
ROWS = 8
HALF = 8
SLOTS = 16
NONE = ROWS * SLOTS
DIST = 4
PAIRS = ((0, 0), (0, -1), (0, -DIST), (1, -1), (-1, -DIST))


def lookup_table(tile_cols, rep, row, blocks):
    cols = {
        d: lax.dynamic_slice_in_dim(
            tile_cols, lax.rem(row + d + blocks, blocks) * ROWS, ROWS, 0
        )
        for d in (0, -1, 1, -DIST)
    }
    place = (jnp.arange(ROWS)[:, None] * SLOTS + jnp.arange(SLOTS)[None, :]).astype(jnp.int32)
    tables = []
    for block_i, block_k in PAIRS:
        named = lax.dynamic_slice_in_dim(cols[block_k], rep * HALF, HALF, 1)
        own = lax.rem(row + block_k + blocks, blocks) * ROWS + jnp.arange(ROWS)
        wanted = jnp.concatenate([own[:, None].astype(jnp.int32), named], axis=1)
        same = (wanted[:, None, :, None] == cols[block_i][None, :, None, :]) & (
            wanted >= 0
        )[:, None, :, None]
        found = jnp.max(jnp.where(same, place[None, :, None, :], -1), axis=-1)
        tables.append(jnp.where(found < 0, NONE, found))
    return jnp.stack(tables).reshape(len(PAIRS) * ROWS, ROWS * (1 + HALF))


def kernel(
    blocks,
    table,
    tiles,
    out,
    own,
    before,
    after,
    far,
    acc,
    given,
    got,
    local_sem,
    pair_send,
    pair_recv,
    far_send,
    far_recv,
    before_send,
    before_recv,
    after_send,
    after_recv,
    pass_before_send,
    pass_before_recv,
    pass_after_send,
    pass_after_recv,
    sum_send,
    sum_recv,
):
    rep = lax.axis_index("rep")
    row = lax.axis_index("row")
    other = 1 - rep
    y = lax.rem(row, DIST)
    last_y = y == DIST - 1
    first_y = y == 0

    def at(step):
        return lax.rem(row + step + blocks, blocks)

    barrier = pltpu.get_barrier_semaphore()

    def greet(device):
        pl.semaphore_signal(barrier, inc=1, device_id=device, device_id_type=MESH)

    greet((other, row))
    for step in (1, -1):
        greet((rep, at(step)))
        greet((other, at(step)))
    for step in (DIST, -DIST):
        greet((rep, at(step)))

    @pl.when(last_y)
    def _():
        greet((rep, at(1 - DIST)))

    @pl.when(first_y)
    def _():
        greet((rep, at(DIST - 1)))

    def mine(c, count=HALF, skip=0):
        return pl.ds(c * SLOTS + rep * HALF + skip, count)

    def load(c):
        return pltpu.make_async_copy(tiles.at[c], own.at[mine(c)], local_sem.at[c])

    def to_partner(c):
        return pltpu.make_async_remote_copy(
            tiles.at[c], own.at[mine(c)], pair_send.at[c], pair_recv.at[c],
            device_id=(other, row), device_id_type=MESH,
        )

    def to_far(c, h):
        return pltpu.make_async_remote_copy(
            tiles.at[c, pl.ds(h * 4, 4)], far.at[c, pl.ds(h * 4, 4)],
            far_send.at[2 * c + h], far_recv.at[2 * c + h],
            device_id=(rep, at(DIST)), device_id_type=MESH,
        )

    def to_next(c, h):
        return pltpu.make_async_remote_copy(
            tiles.at[c, pl.ds(h * 4, 4)], before.at[mine(c, 4, h * 4)],
            before_send.at[2 * c + h], before_recv.at[2 * c + h],
            device_id=(rep, at(1)), device_id_type=MESH,
        )

    def relay(c, h):
        return pltpu.make_async_remote_copy(
            far.at[c, pl.ds(h * 4, 4)], before.at[mine(c, 4, h * 4)],
            before_send.at[2 * c + h], before_recv.at[2 * c + h],
            device_id=(rep, at(1 - DIST)), device_id_type=MESH,
        )

    def to_previous(c):
        return pltpu.make_async_remote_copy(
            tiles.at[c], after.at[mine(c)], after_send.at[c], after_recv.at[c],
            device_id=(rep, at(-1)), device_id_type=MESH,
        )

    def pass_before(c):
        return pltpu.make_async_remote_copy(
            before.at[mine(c)], before.at[mine(c)],
            pass_before_send.at[c], pass_before_recv.at[c],
            device_id=(other, row), device_id_type=MESH,
        )

    def pass_after(c):
        return pltpu.make_async_remote_copy(
            after.at[mine(c)], after.at[mine(c)],
            pass_after_send.at[c], pass_after_recv.at[c],
            device_id=(other, row), device_id_type=MESH,
        )

    for c in range(ROWS):
        load(c).start()
    zero = jnp.zeros((128, 128), jnp.bfloat16)
    for ref in (own, before, after):
        ref[NONE] = zero
    acc[...] = jnp.zeros_like(acc)

    edge = jnp.logical_or(first_y, last_y).astype(jnp.int32)
    pl.semaphore_wait(barrier, 7 + edge)

    @pl.loop(0, ROWS)
    def _(c):
        for h in range(2):
            to_far(c, h).start()

            @pl.when(jnp.logical_not(last_y))
            def _():
                to_next(c, h).start()

        to_previous(c).start()
        to_partner(c).start()

    @pl.loop(0, ROWS)
    def _(c):
        load(c).wait()
        to_partner(c).wait()

    def combine(pair, rows_i, tiles_k, total, c):
        right = jnp.concatenate(tiles_k, axis=1)
        for i in range(ROWS):
            at_i = i * (1 + HALF)
            left = rows_i[table[pair * ROWS + c, at_i]]
            product = jnp.dot(left, right, preferred_element_type=jnp.float32)
            here = acc[total * ROWS + i]
            for s in range(HALF):
                weight = rows_i[table[pair * ROWS + c, at_i + 1 + s]]
                here += product[:, s * 128 : s * 128 + 128] * weight.astype(jnp.float32)
            acc[total * ROWS + i] = here

    def half_row(ref, c):
        return [ref[c * SLOTS + rep * HALF + s] for s in range(HALF)]

    @pl.loop(0, ROWS)
    def _(c):
        for h in range(2):
            to_far(c, h).wait_recv()

            @pl.when(last_y)
            def _():
                relay(c, h).start()

        to_previous(c).wait_recv()
        pass_after(c).start()
        for h in range(2):
            to_next(c, h).wait_recv()
        pass_before(c).start()
        combine(0, own, half_row(own, c), 0, c)
        combine(2, own, [far[c, s] for s in range(HALF)], 0, c)
        combine(1, own, half_row(before, c), 0, c)

    @pl.loop(0, ROWS)
    def _(c):
        pass_after(c).wait()
        pass_before(c).wait()

    @pl.loop(0, ROWS)
    def _(c):
        combine(3, after, half_row(before, c), 1, c)
        combine(4, before, [far[c, s] for s in range(HALF)], 2, c)

    for t in range(3):
        given[t] = jnp.sum(acc[t * ROWS : t * ROWS + ROWS], axis=-1)

    sums = []
    for slot, (source, device) in enumerate(
        (
            (0, (other, row)),
            (1, (rep, at(1))),
            (1, (other, at(1))),
            (2, (rep, at(-1))),
            (2, (other, at(-1))),
        )
    ):
        sums.append(
            pltpu.make_async_remote_copy(
                given.at[source], got.at[slot], sum_send.at[slot], sum_recv.at[slot],
                device_id=device, device_id_type=MESH,
            )
        )
    for copy in sums:
        copy.start()
    for copy in sums:
        copy.wait()
    total = given[0]
    for slot in range(5):
        total += got[slot]
    out[...] = jnp.where(rep == 0, total[:, :64], total[:, 64:])

    @pl.loop(0, ROWS)
    def _(c):
        for h in range(2):
            to_far(c, h).wait_send()
            to_next(c, h).wait_send()
        to_previous(c).wait_send()


def body(blocks, tiles, tile_cols):
    rep = lax.axis_index("rep")
    row = lax.axis_index("row")
    table = lookup_table(tile_cols, rep, row, blocks)
    dma = pltpu.SemaphoreType.DMA
    tile = (128, 128)
    return pl.pallas_call(
        functools.partial(kernel, blocks),
        out_shape=jax.ShapeDtypeStruct((ROWS, 64), jnp.float32),
        in_specs=[
            pl.BlockSpec(memory_space=pltpu.SMEM),
            pl.BlockSpec(memory_space=pltpu.HBM),
        ],
        out_specs=pl.BlockSpec(memory_space=pltpu.VMEM),
        scratch_shapes=[
            pltpu.VMEM((NONE + 1, *tile), jnp.bfloat16),
            pltpu.VMEM((NONE + 1, *tile), jnp.bfloat16),
            pltpu.VMEM((NONE + 1, *tile), jnp.bfloat16),
            pltpu.VMEM((ROWS, HALF, *tile), jnp.bfloat16),
            pltpu.VMEM((3 * ROWS, *tile), jnp.float32),
            pltpu.VMEM((3, ROWS, 128), jnp.float32),
            pltpu.VMEM((5, ROWS, 128), jnp.float32),
            dma((ROWS,)),
            dma((ROWS,)),
            dma((ROWS,)),
            dma((2 * ROWS,)),
            dma((2 * ROWS,)),
            dma((2 * ROWS,)),
            dma((2 * ROWS,)),
            dma((ROWS,)),
            dma((ROWS,)),
            dma((ROWS,)),
            dma((ROWS,)),
            dma((ROWS,)),
            dma((ROWS,)),
            dma((5,)),
            dma((5,)),
        ],
        compiler_params=pltpu.CompilerParams(
            collective_id=0, has_side_effects=True, vmem_limit_bytes=40 << 20
        ),
        name="triangles",
    )(table, tiles)


def solution(mesh):
    return jax.shard_map(
        functools.partial(body, mesh.shape["row"]),
        mesh=mesh,
        in_specs=(P("row", "rep", None, None), P()),
        out_specs=P("row", "rep"),
        check_vma=False,
    )
```

```python
import functools

import jax
import jax.numpy as jnp
from jax import lax
from jax.experimental import pallas as pl
from jax.experimental.pallas import tpu as pltpu
from jax.sharding import PartitionSpec as P

MESH = pl.DeviceIdType.MESH
TILE = 128
ROWS = 8
HALF = 8
SLOTS = 16
NONE = ROWS * SLOTS
DIST = 4
PIECES = 4
PIECE = HALF // PIECES
PAIRS = ((0, 0), (0, -1), (0, -DIST), (1, -1), (-1, -DIST))
GROUPS = ((0, 3), (3, 3), (6, 1), (7, 1))


def group_of(c):
    return next(g for g, (first, size) in enumerate(GROUPS) if first <= c < first + size)


def kernel(
    blocks,
    cols_hbm,
    tiles,
    out,
    own,
    before,
    far,
    after_0,
    after_1,
    after_2,
    after_3,
    prior_0,
    prior_1,
    prior_2,
    prior_3,
    acc,
    given,
    got,
    cols,
    found,
    table,
    local_sem,
    keep_sem,
    cols_sem,
    table_sem,
    pair_send,
    pair_recv,
    far_send,
    far_recv,
    before_send,
    before_recv,
    after_send,
    after_recv,
    pass_before_send,
    pass_before_recv,
    pass_after_send,
    pass_after_recv,
    sum_send,
    sum_recv,
):
    after = (after_0, after_1, after_2, after_3)
    prior = (prior_0, prior_1, prior_2, prior_3)
    rep = lax.axis_index("rep")
    row = lax.axis_index("row")
    other = 1 - rep
    y = lax.rem(row, DIST)
    last_y = y == DIST - 1
    first_y = y == 0

    def at(step):
        return lax.rem(row + step + blocks, blocks)

    barrier = pltpu.get_barrier_semaphore()

    def greet(device):
        pl.semaphore_signal(barrier, inc=1, device_id=device, device_id_type=MESH)

    greet((other, row))
    for step in (1, -1):
        greet((rep, at(step)))
        greet((other, at(step)))
    for step in (DIST, -DIST):
        greet((rep, at(step)))

    @pl.when(last_y)
    def _():
        greet((rep, at(1 - DIST)))

    @pl.when(first_y)
    def _():
        greet((rep, at(DIST - 1)))

    def remote(source, target, send, recv, device):
        return pltpu.make_async_remote_copy(
            source, target, send, recv, device_id=device, device_id_type=MESH
        )

    def load(c):
        return pltpu.make_async_copy(
            tiles.at[c], own.at[pl.ds(c * SLOTS + rep * HALF, HALF)], local_sem.at[c]
        )

    def to_partner(c):
        return remote(
            tiles.at[c], own.at[pl.ds(c * SLOTS + rep * HALF, HALF)],
            pair_send.at[c], pair_recv.at[c], (other, row),
        )

    def to_far(c, h):
        piece = pl.ds(h * PIECE, PIECE)
        place = c * PIECES + h
        return remote(
            tiles.at[c, piece], far.at[c, piece],
            far_send.at[place], far_recv.at[place], (rep, at(DIST)),
        )

    def to_next(c, h):
        piece = pl.ds(h * PIECE, PIECE)
        place = c * PIECES + h
        return remote(
            tiles.at[c, piece], before.at[c, piece],
            before_send.at[place], before_recv.at[place], (rep, at(1)),
        )

    def relay(c, h):
        piece = pl.ds(h * PIECE, PIECE)
        place = c * PIECES + h
        return remote(
            far.at[c, piece], before.at[c, piece],
            before_send.at[place], before_recv.at[place], (rep, at(1 - DIST)),
        )

    def half_of(g, c):
        return pl.ds((c - GROUPS[g][0]) * SLOTS + rep * HALF, HALF)

    def to_previous(g, c):
        return remote(
            tiles.at[c], after[g].at[half_of(g, c)],
            after_send.at[c], after_recv.at[c], (rep, at(-1)),
        )

    def pass_after(g, c):
        return remote(
            after[g].at[half_of(g, c)], after[g].at[half_of(g, c)],
            pass_after_send.at[c], pass_after_recv.at[c], (other, row),
        )

    def pass_before(g, c):
        return remote(
            before.at[c], prior[g].at[half_of(g, c)],
            pass_before_send.at[c], pass_before_recv.at[c], (other, row),
        )

    def keep_before(g, c):
        return pltpu.make_async_copy(before.at[c], prior[g].at[half_of(g, c)], keep_sem.at[c])

    def per_group(c, action):
        for g, (first, size) in enumerate(GROUPS):

            @pl.when(jnp.logical_and(c >= first, c < first + size))
            def _():
                action(g)

    fetch = pltpu.make_async_copy(cols_hbm, cols, cols_sem)
    fetch.start()
    for c in range(ROWS):
        load(c).start()

    edge = jnp.logical_or(first_y, last_y).astype(jnp.int32)
    pl.semaphore_wait(barrier, 7 + edge)

    for c in range(ROWS):
        for h in range(PIECES):
            to_far(c, h).start()

            @pl.when(jnp.logical_not(last_y))
            def _():
                to_next(c, h).start()

        to_previous(group_of(c), c).start()
        to_partner(c).start()

    fetch.wait()
    known = cols[...].astype(jnp.float32)
    vertex = lax.broadcasted_iota(jnp.int32, (blocks * ROWS, TILE), 0)
    lane = lax.broadcasted_iota(jnp.int32, (blocks * ROWS, TILE), 1)

    def columns_at(wanted):
        pick = (vertex == wanted).astype(jnp.float32)
        return jnp.dot(
            known, pick, precision=lax.Precision.HIGHEST, preferred_element_type=jnp.float32
        ).astype(jnp.int32)

    of_k = {}
    for step in (0, -1, -DIST):
        both = columns_at(at(step) * ROWS + lane % ROWS)
        of_k[step] = jnp.where(rep == 0, both[:HALF], both[HALF:])
    of_i = {step: columns_at(at(step) * ROWS + lane // ROWS) for step in (0, 1, -1)}
    lane = lax.broadcasted_iota(jnp.int32, (HALF, TILE), 1)
    index_i = lane // ROWS
    first = jnp.zeros_like(lane)
    size = jnp.ones_like(lane)
    for begin, count in GROUPS:
        inside = index_i >= begin
        first = jnp.where(inside, begin, first)
        size = jnp.where(inside, count, size)
    for pair, (step_i, step_k) in enumerate(PAIRS):
        if step_i == 0:
            base, none = index_i * SLOTS, jnp.full_like(lane, NONE)
        else:
            base, none = (index_i - first) * SLOTS, size * SLOTS
        own_col = at(step_k) * ROWS + lane % ROWS
        for part, wanted in enumerate((of_k[step_k], own_col)):
            place = none
            for s in range(SLOTS):
                same = jnp.logical_and(wanted == of_i[step_i][s : s + 1], wanted >= 0)
                place = jnp.where(same, base + s, place)
            found[pair * SLOTS + part * HALF : pair * SLOTS + part * HALF + HALF] = place

    zero = jnp.zeros((TILE, TILE), jnp.bfloat16)
    own[NONE] = zero
    for g, (_, count) in enumerate(GROUPS):
        after[g][count * SLOTS] = zero
        prior[g][count * SLOTS] = zero
    acc[...] = jnp.zeros_like(acc)
    spread = pltpu.make_async_copy(found, table, table_sem)
    spread.start()

    @pl.loop(0, ROWS)
    def _(c):
        load(c).wait()
        to_partner(c).wait()

    spread.wait()

    def combine(pair, rows_i, tiles_k, total, c, members=range(ROWS)):
        right = jnp.concatenate(tiles_k, axis=1)
        for i in members:
            column = i * ROWS + c
            left = rows_i[table[pair * SLOTS + HALF, column]]
            product = jnp.dot(left, right, preferred_element_type=jnp.float32)
            here = acc[total * ROWS + i]
            for s in range(HALF):
                weight = rows_i[table[pair * SLOTS + s, column]]
                here += product[:, s * TILE : s * TILE + TILE] * weight.astype(jnp.float32)
            acc[total * ROWS + i] = here

    def row_of(ref, c):
        return [ref[c, s] for s in range(HALF)]

    def own_pairs(c):
        combine(2, own, row_of(far, c), 0, c)
        combine(1, own, row_of(before, c), 0, c)

    def away_pairs(g, c):
        members = range(GROUPS[g][0], GROUPS[g][0] + GROUPS[g][1])
        combine(3, after[g], row_of(before, c), 1, c, members)
        combine(4, prior[g], row_of(far, c), 2, c, members)

    def complete(g):
        for c in range(GROUPS[g][0], GROUPS[g][0] + GROUPS[g][1]):
            pass_after(g, c).wait_recv()
            pass_before(g, c).wait_recv()
            keep_before(g, c).wait()

    last = ROWS - 1

    @pl.loop(0, ROWS)
    def _(c):
        for h in range(PIECES):
            to_far(c, h).wait_recv()

            @pl.when(last_y)
            def _():
                relay(c, h).start()

        def on_after(g):
            to_previous(g, c).wait_recv()
            pass_after(g, c).start()

        per_group(c, on_after)
        for h in range(PIECES):
            to_next(c, h).wait_recv()

        def on_before(g):
            pass_before(g, c).start()
            keep_before(g, c).start()

        per_group(c, on_before)

        @pl.when(c < last)
        def _():
            @pl.loop(0, jnp.where(c == 3, 2, 1))
            def _(again):
                k = c + again * DIST
                combine(0, own, [own[k * SLOTS + rep * HALF + s] for s in range(HALF)], 0, k)

            own_pairs(c)

        for g in (0, 1):
            end = GROUPS[g][0] + GROUPS[g][1] - 1

            @pl.when(c == end)
            def _():
                complete(g)

            @pl.when(c >= end)
            def _():
                @pl.loop(jnp.where(c == end, 0, c), c + 1)
                def _(k):
                    away_pairs(g, k)

        @pl.when(c == last - 1)
        def _():
            complete(2)

        @pl.when(c >= last - 1)
        def _():
            late = c - (last - 1)

            @pl.loop(late * 3, 3 + late)
            def _(k):
                away_pairs(2, 2 * k)
                away_pairs(2, 2 * k + 1)

    complete(3)

    @pl.loop(0, ROWS // 2)
    def _(k):
        away_pairs(3, 2 * k)
        away_pairs(3, 2 * k + 1)

    def sum_copy(slot, source, device):
        return remote(given.at[source], got.at[slot], sum_send.at[slot], sum_recv.at[slot], device)

    def add_up(t):
        given[t] = jnp.sum(acc[t * ROWS : t * ROWS + ROWS], axis=-1)

    sums = [
        sum_copy(1, 1, (rep, at(1))),
        sum_copy(2, 1, (other, at(1))),
        sum_copy(3, 2, (rep, at(-1))),
        sum_copy(4, 2, (other, at(-1))),
    ]
    add_up(1)
    add_up(2)
    for copy in sums:
        copy.start()
    own_pairs(last)
    add_up(0)
    sums.append(sum_copy(0, 0, (other, row)))
    sums[-1].start()
    for copy in sums:
        copy.wait()
    total = given[0]
    for slot in range(5):
        total += got[slot]
    out[...] = jnp.where(rep == 0, total[:, : TILE // 2], total[:, TILE // 2 :])

    for c in range(ROWS):
        for h in range(PIECES):
            to_far(c, h).wait_send()
            to_next(c, h).wait_send()
        g = group_of(c)
        to_previous(g, c).wait_send()
        pass_after(g, c).wait_send()
        pass_before(g, c).wait_send()


def body(blocks, tiles, tile_cols):
    dma = pltpu.SemaphoreType.DMA

    def stack(count):
        return pltpu.VMEM((count, TILE, TILE), jnp.bfloat16)

    half = pltpu.VMEM((ROWS, HALF, TILE, TILE), jnp.bfloat16)
    groups = [stack(count * SLOTS + 1) for _, count in GROUPS]
    pieces = ROWS * PIECES
    return pl.pallas_call(
        functools.partial(kernel, blocks),
        out_shape=jax.ShapeDtypeStruct((ROWS, TILE // 2), jnp.float32),
        in_specs=[
            pl.BlockSpec(memory_space=pltpu.HBM),
            pl.BlockSpec(memory_space=pltpu.HBM),
        ],
        out_specs=pl.BlockSpec(memory_space=pltpu.VMEM),
        scratch_shapes=[
            stack(NONE + 1),
            half,
            half,
            *groups,
            *groups,
            pltpu.VMEM((3 * ROWS, TILE, TILE), jnp.float32),
            pltpu.VMEM((3, ROWS, TILE), jnp.float32),
            pltpu.VMEM((5, ROWS, TILE), jnp.float32),
            pltpu.VMEM((SLOTS, blocks * ROWS), jnp.int32),
            pltpu.VMEM((len(PAIRS) * SLOTS, TILE), jnp.int32),
            pltpu.SMEM((len(PAIRS) * SLOTS, TILE), jnp.int32),
            dma((ROWS,)),
            dma((ROWS,)),
            dma,
            dma,
            dma((ROWS,)),
            dma((ROWS,)),
            dma((pieces,)),
            dma((pieces,)),
            dma((pieces,)),
            dma((pieces,)),
            dma((ROWS,)),
            dma((ROWS,)),
            dma((ROWS,)),
            dma((ROWS,)),
            dma((ROWS,)),
            dma((ROWS,)),
            dma((5,)),
            dma((5,)),
        ],
        compiler_params=pltpu.CompilerParams(
            collective_id=0, has_side_effects=True, vmem_limit_bytes=67_030_000
        ),
        name="triangles",
    )(tile_cols.T, tiles)


def solution(mesh):
    return jax.shard_map(
        functools.partial(body, mesh.shape["row"]),
        mesh=mesh,
        in_specs=(P("row", "rep", None, None), P()),
        out_specs=P("row", "rep"),
        check_vma=False,
    )
```

```python
import functools

import jax
import jax.numpy as jnp
from jax import lax
from jax.experimental import pallas as pl
from jax.experimental.pallas import tpu as pltpu
from jax.sharding import PartitionSpec as P

MESH = pl.DeviceIdType.MESH
TILE = 128
ROWS = 8
HALF = 8
SLOTS = 16
NONE = ROWS * SLOTS
DIST = 4
PIECES = 4
PIECE = HALF // PIECES
PAIRS = ((0, 0), (0, -1), (0, -DIST), (1, -1), (-1, -DIST))
GROUPS = ((0, 3), (3, 3), (6, 1), (7, 1))


def group_of(c):
    return next(g for g, (first, size) in enumerate(GROUPS) if first <= c < first + size)


def kernel(
    blocks,
    cols_hbm,
    tiles,
    out,
    own,
    before,
    far,
    after_0,
    after_1,
    after_2,
    after_3,
    prior_0,
    prior_1,
    prior_2,
    prior_3,
    acc,
    given,
    got,
    cols,
    of_k,
    of_i,
    found,
    table,
    local_sem,
    keep_sem,
    cols_sem,
    table_sem,
    pair_send,
    pair_recv,
    far_send,
    far_recv,
    before_send,
    before_recv,
    after_send,
    after_recv,
    pass_before_send,
    pass_before_recv,
    pass_after_send,
    pass_after_recv,
    sum_send,
    sum_recv,
):
    after = (after_0, after_1, after_2, after_3)
    prior = (prior_0, prior_1, prior_2, prior_3)
    rep = lax.axis_index("rep")
    row = lax.axis_index("row")
    other = 1 - rep
    y = lax.rem(row, DIST)
    last_y = y == DIST - 1
    first_y = y == 0

    def at(step):
        return lax.rem(row + step + blocks, blocks)

    barrier = pltpu.get_barrier_semaphore()

    def greet(device):
        pl.semaphore_signal(barrier, inc=1, device_id=device, device_id_type=MESH)

    greet((other, row))
    for step in (1, -1):
        greet((rep, at(step)))
        greet((other, at(step)))
    for step in (DIST, -DIST):
        greet((rep, at(step)))

    @pl.when(last_y)
    def _():
        greet((rep, at(1 - DIST)))

    @pl.when(first_y)
    def _():
        greet((rep, at(DIST - 1)))

    def remote(source, target, send, recv, device):
        return pltpu.make_async_remote_copy(
            source, target, send, recv, device_id=device, device_id_type=MESH
        )

    def load(c):
        return pltpu.make_async_copy(
            tiles.at[c], own.at[pl.ds(c * SLOTS + rep * HALF, HALF)], local_sem.at[c]
        )

    def to_partner(c):
        return remote(
            tiles.at[c], own.at[pl.ds(c * SLOTS + rep * HALF, HALF)],
            pair_send.at[c], pair_recv.at[c], (other, row),
        )

    def to_far(c, h):
        piece = pl.ds(h * PIECE, PIECE)
        place = c * PIECES + h
        return remote(
            tiles.at[c, piece], far.at[c, piece],
            far_send.at[place], far_recv.at[place], (rep, at(DIST)),
        )

    def to_next(c, h):
        piece = pl.ds(h * PIECE, PIECE)
        place = c * PIECES + h
        return remote(
            tiles.at[c, piece], before.at[c, piece],
            before_send.at[place], before_recv.at[place], (rep, at(1)),
        )

    def relay(c, h):
        piece = pl.ds(h * PIECE, PIECE)
        place = c * PIECES + h
        return remote(
            far.at[c, piece], before.at[c, piece],
            before_send.at[place], before_recv.at[place], (rep, at(1 - DIST)),
        )

    def half_of(g, c):
        return pl.ds((c - GROUPS[g][0]) * SLOTS + rep * HALF, HALF)

    def to_previous(g, c):
        return remote(
            tiles.at[c], after[g].at[half_of(g, c)],
            after_send.at[c], after_recv.at[c], (rep, at(-1)),
        )

    def pass_after(g, c):
        return remote(
            after[g].at[half_of(g, c)], after[g].at[half_of(g, c)],
            pass_after_send.at[c], pass_after_recv.at[c], (other, row),
        )

    def pass_before(g, c):
        return remote(
            before.at[c], prior[g].at[half_of(g, c)],
            pass_before_send.at[c], pass_before_recv.at[c], (other, row),
        )

    def keep_before(g, c):
        return pltpu.make_async_copy(before.at[c], prior[g].at[half_of(g, c)], keep_sem.at[c])

    def per_group(c, action):
        for g, (first, size) in enumerate(GROUPS):

            @pl.when(jnp.logical_and(c >= first, c < first + size))
            def _():
                action(g)

    fetch = pltpu.make_async_copy(cols_hbm, cols, cols_sem)
    fetch.start()
    for c in range(ROWS):
        load(c).start()

    edge = jnp.logical_or(first_y, last_y).astype(jnp.int32)
    pl.semaphore_wait(barrier, 7 + edge)

    for c in range(ROWS):
        for h in range(PIECES):
            to_far(c, h).start()

            @pl.when(jnp.logical_not(last_y))
            def _():
                to_next(c, h).start()

        to_previous(group_of(c), c).start()
        to_partner(c).start()

    def relay_piece(c, h):
        to_far(c, h).wait_recv()

        @pl.when(last_y)
        def _():
            relay(c, h).start()

    fetch.wait()
    known = cols[...].astype(jnp.float32)
    vertex = lax.broadcasted_iota(jnp.int32, (blocks * ROWS, TILE), 0)
    lane = lax.broadcasted_iota(jnp.int32, (blocks * ROWS, TILE), 1)

    def columns_at(wanted):
        pick = (vertex == wanted).astype(jnp.float32)
        return jnp.dot(
            known, pick, precision=lax.Precision.HIGHEST, preferred_element_type=jnp.float32
        ).astype(jnp.int32)

    for t, step in enumerate((0, -1, -DIST)):
        both = columns_at(at(step) * ROWS + lane % ROWS)
        of_k[t] = jnp.where(rep == 0, both[:HALF], both[HALF:])
    relay_piece(0, 0)
    for t, step in enumerate((0, 1, -1)):
        of_i[t] = columns_at(at(step) * ROWS + lane // ROWS)
    relay_piece(0, 1)
    lane = lax.broadcasted_iota(jnp.int32, (HALF, TILE), 1)
    index_i = lane // ROWS
    first = jnp.zeros_like(lane)
    size = jnp.ones_like(lane)
    for begin, count in GROUPS:
        inside = index_i >= begin
        first = jnp.where(inside, begin, first)
        size = jnp.where(inside, count, size)
    for pair, (step_i, step_k) in enumerate(PAIRS):
        if step_i == 0:
            base, none = index_i * SLOTS, jnp.full_like(lane, NONE)
        else:
            base, none = (index_i - first) * SLOTS, size * SLOTS
        own_col = at(step_k) * ROWS + lane % ROWS
        named = of_k[(0, -1, -DIST).index(step_k)]
        held = of_i[(0, 1, -1).index(step_i)]
        for part, wanted in enumerate((named, own_col)):
            place = none
            for s in range(SLOTS):
                same = jnp.logical_and(wanted == held[s : s + 1], wanted >= 0)
                place = jnp.where(same, base + s, place)
            found[pair * SLOTS + part * HALF : pair * SLOTS + part * HALF + HALF] = place
    relay_piece(0, 2)
    zero = jnp.zeros((TILE, TILE), jnp.bfloat16)
    own[NONE] = zero
    for g, (_, count) in enumerate(GROUPS):
        after[g][count * SLOTS] = zero
        prior[g][count * SLOTS] = zero
    acc[...] = jnp.zeros_like(acc)
    spread = pltpu.make_async_copy(found, table, table_sem)
    spread.start()
    relay_piece(0, 3)

    def combine(pair, rows_i, tiles_k, total, c, members=range(ROWS)):
        right = jnp.concatenate(tiles_k, axis=1)
        for i in members:
            column = i * ROWS + c
            left = rows_i[table[pair * SLOTS + HALF, column]]
            product = jnp.dot(left, right, preferred_element_type=jnp.float32)
            here = acc[total * ROWS + i]
            for s in range(HALF):
                weight = rows_i[table[pair * SLOTS + s, column]]
                here += product[:, s * TILE : s * TILE + TILE] * weight.astype(jnp.float32)
            acc[total * ROWS + i] = here

    def row_of(ref, c):
        return [ref[c, s] for s in range(HALF)]

    def own_pairs(c):
        combine(2, own, row_of(far, c), 0, c)
        combine(1, own, row_of(before, c), 0, c)

    def away_pairs(g, c):
        members = range(GROUPS[g][0], GROUPS[g][0] + GROUPS[g][1])
        combine(3, after[g], row_of(before, c), 1, c, members)
        combine(4, prior[g], row_of(far, c), 2, c, members)

    def complete(g):
        for c in range(GROUPS[g][0], GROUPS[g][0] + GROUPS[g][1]):
            pass_after(g, c).wait_recv()
            pass_before(g, c).wait_recv()
            keep_before(g, c).wait()

    last = ROWS - 1

    def arrivals(c):
        def on_after(g):
            to_previous(g, c).wait_recv()
            pass_after(g, c).start()

        per_group(c, on_after)
        for h in range(PIECES):
            to_next(c, h).wait_recv()

        def on_before(g):
            pass_before(g, c).start()
            keep_before(g, c).start()

        per_group(c, on_before)

    def spans(p, *entries):
        begin, end = 0, 0
        for when, low, high in entries:
            begin = jnp.where(when, low, begin)
            end = jnp.where(when, high, end)
        return begin, end

    @pl.loop(PIECES, ROWS * PIECES)
    def _(p):
        c = p // PIECES
        h = lax.rem(p, PIECES)
        relay_piece(c, h)

        @pl.when(h == 0)
        def _():
            arrivals(c - 1)

        @pl.when(p == 2 * PIECES)
        def _():
            @pl.loop(0, ROWS)
            def _(k):
                load(k).wait()
                to_partner(k).wait()

            spread.wait()

        def both(*tests):
            return functools.reduce(jnp.logical_and, tests)

        begin, end = spans(
            p,
            (both(h == 0, c >= 2), c - 1, c),
            (p == 11, 0, 1),
        )

        @pl.loop(begin, end)
        def _(k):
            own_pairs(k)

        begin, end = spans(p, (both(h == 1, c >= 2, c <= 5), 2 * c - 4, 2 * c - 2))

        @pl.loop(begin, end)
        def _(k):
            combine(0, own, [own[k * SLOTS + rep * HALF + s] for s in range(HALF)], 0, k)

        @pl.when(p == 14)
        def _():
            complete(0)

        begin, end = spans(
            p, (both(h == 2, c >= 4), c - 1, c), (p == 14, 0, 2), (p == 15, 2, 3)
        )

        @pl.loop(begin, end)
        def _(k):
            away_pairs(0, k)

        @pl.when(p == 25)
        def _():
            complete(1)

        begin, end = spans(
            p, (p == 25, 0, 2), (p == 26, 2, 4), (p == 27, 4, 6), (p == 30, 6, 7)
        )

        @pl.loop(begin, end)
        def _(k):
            away_pairs(1, k)

        @pl.when(p == 29)
        def _():
            complete(2)

        begin, end = spans(p, (p == 29, 0, 2), (p == 31, 2, 3))

        @pl.loop(begin, end)
        def _(k):
            away_pairs(2, 2 * k)
            away_pairs(2, 2 * k + 1)

    arrivals(last)
    away_pairs(0, last)
    away_pairs(1, last)
    away_pairs(2, last - 1)
    away_pairs(2, last)
    complete(3)

    @pl.loop(0, ROWS // 2)
    def _(k):
        away_pairs(3, 2 * k)
        away_pairs(3, 2 * k + 1)

    def sum_copy(slot, source, device):
        return remote(given.at[source], got.at[slot], sum_send.at[slot], sum_recv.at[slot], device)

    def add_up(t):
        given[t] = jnp.sum(acc[t * ROWS : t * ROWS + ROWS], axis=-1)

    sums = [
        sum_copy(1, 1, (rep, at(1))),
        sum_copy(2, 1, (other, at(1))),
        sum_copy(3, 2, (rep, at(-1))),
        sum_copy(4, 2, (other, at(-1))),
    ]
    add_up(1)
    add_up(2)
    for copy in sums:
        copy.start()
    own_pairs(last)
    add_up(0)
    sums.append(sum_copy(0, 0, (other, row)))
    sums[-1].start()
    for copy in sums:
        copy.wait()
    total = given[0]
    for slot in range(5):
        total += got[slot]
    out[...] = jnp.where(rep == 0, total[:, : TILE // 2], total[:, TILE // 2 :])

    for c in range(ROWS):
        for h in range(PIECES):
            to_far(c, h).wait_send()
            to_next(c, h).wait_send()
        g = group_of(c)
        to_previous(g, c).wait_send()
        pass_after(g, c).wait_send()
        pass_before(g, c).wait_send()


def body(blocks, tiles, tile_cols):
    dma = pltpu.SemaphoreType.DMA

    def stack(count):
        return pltpu.VMEM((count, TILE, TILE), jnp.bfloat16)

    half = pltpu.VMEM((ROWS, HALF, TILE, TILE), jnp.bfloat16)
    groups = [stack(count * SLOTS + 1) for _, count in GROUPS]
    pieces = ROWS * PIECES
    return pl.pallas_call(
        functools.partial(kernel, blocks),
        out_shape=jax.ShapeDtypeStruct((ROWS, TILE // 2), jnp.float32),
        in_specs=[
            pl.BlockSpec(memory_space=pltpu.HBM),
            pl.BlockSpec(memory_space=pltpu.HBM),
        ],
        out_specs=pl.BlockSpec(memory_space=pltpu.VMEM),
        scratch_shapes=[
            stack(NONE + 1),
            half,
            half,
            *groups,
            *groups,
            pltpu.VMEM((3 * ROWS, TILE, TILE), jnp.float32),
            pltpu.VMEM((3, ROWS, TILE), jnp.float32),
            pltpu.VMEM((5, ROWS, TILE), jnp.float32),
            pltpu.VMEM((SLOTS, blocks * ROWS), jnp.int32),
            pltpu.VMEM((3, HALF, TILE), jnp.int32),
            pltpu.VMEM((3, SLOTS, TILE), jnp.int32),
            pltpu.VMEM((len(PAIRS) * SLOTS, TILE), jnp.int32),
            pltpu.SMEM((len(PAIRS) * SLOTS, TILE), jnp.int32),
            dma((ROWS,)),
            dma((ROWS,)),
            dma,
            dma,
            dma((ROWS,)),
            dma((ROWS,)),
            dma((pieces,)),
            dma((pieces,)),
            dma((pieces,)),
            dma((pieces,)),
            dma((ROWS,)),
            dma((ROWS,)),
            dma((ROWS,)),
            dma((ROWS,)),
            dma((ROWS,)),
            dma((ROWS,)),
            dma((5,)),
            dma((5,)),
        ],
        compiler_params=pltpu.CompilerParams(
            collective_id=0, has_side_effects=True, vmem_limit_bytes=67_030_000
        ),
        name="triangles",
    )(tile_cols.T, tiles)


def solution(mesh):
    return jax.shard_map(
        functools.partial(body, mesh.shape["row"]),
        mesh=mesh,
        in_specs=(P("row", "rep", None, None), P()),
        out_specs=P("row", "rep"),
        check_vma=False,
    )
```

```python
import functools

import jax
import jax.numpy as jnp
from jax import lax
from jax.experimental import pallas as pl
from jax.experimental.pallas import tpu as pltpu
from jax.sharding import PartitionSpec as P

MESH = pl.DeviceIdType.MESH
TILE = 128
ROWS = 8
HALF = 8
SLOTS = 16
NONE = ROWS * SLOTS
DIST = 4
PIECES = 4
PIECE = HALF // PIECES
PAIRS = ((0, 0), (0, -1), (0, -DIST), (1, -1), (-1, -DIST))
GROUPS = ((0, 3), (3, 3), (6, 1), (7, 1))


def group_of(c):
    return next(g for g, (first, size) in enumerate(GROUPS) if first <= c < first + size)


def kernel(
    blocks,
    cols_hbm,
    tiles,
    out,
    own,
    before,
    far,
    after_0,
    after_1,
    after_2,
    after_3,
    prior_0,
    prior_1,
    prior_2,
    prior_3,
    acc,
    given,
    got,
    cols,
    of_k,
    of_i,
    found,
    table,
    local_sem,
    keep_sem,
    cols_sem,
    table_sem,
    fill_sem,
    pair_send,
    pair_recv,
    far_send,
    far_recv,
    before_send,
    before_recv,
    after_send,
    after_recv,
    pass_before_send,
    pass_before_recv,
    pass_after_send,
    pass_after_recv,
    sum_send,
    sum_recv,
    relay_send,
):
    after = (after_0, after_1, after_2, after_3)
    prior = (prior_0, prior_1, prior_2, prior_3)
    rep = lax.axis_index("rep")
    row = lax.axis_index("row")
    other = 1 - rep
    y = lax.rem(row, DIST)
    last_y = y == DIST - 1
    first_y = y == 0
    top = row == blocks - 1
    has_far = jnp.logical_or(row >= DIST, row == 0)
    gives_far = row <= blocks - DIST
    relays = jnp.logical_and(last_y, row >= DIST)
    gives_next = jnp.logical_or(jnp.logical_not(last_y), top)

    def at(step):
        return lax.rem(row + step + blocks, blocks)

    barrier = pltpu.get_barrier_semaphore()

    def greet(device):
        pl.semaphore_signal(barrier, inc=1, device_id=device, device_id_type=MESH)

    greet((other, row))
    for step in (1, -1):
        greet((rep, at(step)))
        greet((other, at(step)))
    for step in (DIST, -DIST):
        greet((rep, at(step)))

    @pl.when(last_y)
    def _():
        greet((rep, at(1 - DIST)))

    @pl.when(first_y)
    def _():
        greet((rep, at(DIST - 1)))

    def remote(source, target, send, recv, device):
        return pltpu.make_async_remote_copy(
            source, target, send, recv, device_id=device, device_id_type=MESH
        )

    def load(c):
        return pltpu.make_async_copy(
            tiles.at[c], own.at[pl.ds(c * SLOTS + rep * HALF, HALF)], local_sem.at[c]
        )

    def to_partner(c):
        return remote(
            tiles.at[c], own.at[pl.ds(c * SLOTS + rep * HALF, HALF)],
            pair_send.at[c], pair_recv.at[c], (other, row),
        )

    def to_far(c, h):
        piece = pl.ds(h * PIECE, PIECE)
        place = c * PIECES + h
        return remote(
            tiles.at[c, piece], far.at[c, piece],
            far_send.at[place], far_recv.at[place], (rep, at(DIST)),
        )

    def to_next(c, h):
        piece = pl.ds(h * PIECE, PIECE)
        place = c * PIECES + h
        return remote(
            tiles.at[c, piece], before.at[c, piece],
            before_send.at[place], before_recv.at[place], (rep, at(1)),
        )

    def relay(c, h):
        piece = pl.ds(h * PIECE, PIECE)
        place = c * PIECES + h
        return remote(
            far.at[c, piece], before.at[c, piece],
            relay_send.at[place], before_recv.at[place], (rep, at(1 - DIST)),
        )

    def half_of(g, c):
        return pl.ds((c - GROUPS[g][0]) * SLOTS + rep * HALF, HALF)

    def to_previous(g, c):
        return remote(
            tiles.at[c], after[g].at[half_of(g, c)],
            after_send.at[c], after_recv.at[c], (rep, at(-1)),
        )

    def pass_after(g, c):
        return remote(
            after[g].at[half_of(g, c)], after[g].at[half_of(g, c)],
            pass_after_send.at[c], pass_after_recv.at[c], (other, row),
        )

    def pass_before(g, c):
        return remote(
            before.at[c], prior[g].at[half_of(g, c)],
            pass_before_send.at[c], pass_before_recv.at[c], (other, row),
        )

    def keep_before(g, c):
        return pltpu.make_async_copy(before.at[c], prior[g].at[half_of(g, c)], keep_sem.at[c])

    def per_group(c, action):
        for g, (first, size) in enumerate(GROUPS):

            @pl.when(jnp.logical_and(c >= first, c < first + size))
            def _():
                action(g)

    fetch = pltpu.make_async_copy(cols_hbm, cols, cols_sem)
    fetch.start()
    for c in range(ROWS):
        load(c).start()

    edge = jnp.logical_or(first_y, last_y).astype(jnp.int32)
    pl.semaphore_wait(barrier, 7 + edge)

    fill = pltpu.make_async_copy(tiles, far, fill_sem)

    @pl.when(jnp.logical_not(has_far))
    def _():
        fill.start()

    for c in range(ROWS):
        for h in range(PIECES):

            @pl.when(gives_far)
            def _():
                to_far(c, h).start()

            @pl.when(gives_next)
            def _():
                to_next(c, h).start()

        to_previous(group_of(c), c).start()
        to_partner(c).start()

    def relay_piece(c, h):
        @pl.when(has_far)
        def _():
            to_far(c, h).wait_recv()

        @pl.when(relays)
        def _():
            relay(c, h).start()

    fetch.wait()
    known = cols[...].astype(jnp.float32)
    vertex = lax.broadcasted_iota(jnp.int32, (blocks * ROWS, TILE), 0)
    lane = lax.broadcasted_iota(jnp.int32, (blocks * ROWS, TILE), 1)

    def columns_at(wanted):
        pick = (vertex == wanted).astype(jnp.float32)
        return jnp.dot(
            known, pick, precision=lax.Precision.HIGHEST, preferred_element_type=jnp.float32
        ).astype(jnp.int32)

    for t, step in enumerate((0, -1, -DIST)):
        both = columns_at(at(step) * ROWS + lane % ROWS)
        of_k[t] = jnp.where(rep == 0, both[:HALF], both[HALF:])
    relay_piece(0, 0)
    for t, step in enumerate((0, 1, -1)):
        of_i[t] = columns_at(at(step) * ROWS + lane // ROWS)
    relay_piece(0, 1)
    lane = lax.broadcasted_iota(jnp.int32, (HALF, TILE), 1)
    index_i = lane // ROWS
    first = jnp.zeros_like(lane)
    size = jnp.ones_like(lane)
    for begin, count in GROUPS:
        inside = index_i >= begin
        first = jnp.where(inside, begin, first)
        size = jnp.where(inside, count, size)
    for pair, (step_i, step_k) in enumerate(PAIRS):
        if step_i == 0:
            base, none = index_i * SLOTS, jnp.full_like(lane, NONE)
        else:
            base, none = (index_i - first) * SLOTS, size * SLOTS
        own_col = at(step_k) * ROWS + lane % ROWS
        named = of_k[(0, -1, -DIST).index(step_k)]
        held = of_i[(0, 1, -1).index(step_i)]
        for part, wanted in enumerate((named, own_col)):
            place = none
            for s in range(SLOTS):
                same = jnp.logical_and(wanted == held[s : s + 1], wanted >= 0)
                place = jnp.where(same, base + s, place)
            found[pair * SLOTS + part * HALF : pair * SLOTS + part * HALF + HALF] = place
    relay_piece(0, 2)
    zero = jnp.zeros((TILE, TILE), jnp.bfloat16)
    own[NONE] = zero
    for g, (_, count) in enumerate(GROUPS):
        after[g][count * SLOTS] = zero
        prior[g][count * SLOTS] = zero
    acc[...] = jnp.zeros_like(acc)
    spread = pltpu.make_async_copy(found, table, table_sem)
    spread.start()
    relay_piece(0, 3)

    def combine(pair, rows_i, tiles_k, total, c, members=range(ROWS)):
        right = jnp.concatenate(tiles_k, axis=1)
        for i in members:
            column = i * ROWS + c
            left = rows_i[table[pair * SLOTS + HALF, column]]
            product = jnp.dot(left, right, preferred_element_type=jnp.float32)
            here = acc[total * ROWS + i]
            for s in range(HALF):
                weight = rows_i[table[pair * SLOTS + s, column]]
                here += product[:, s * TILE : s * TILE + TILE] * weight.astype(jnp.float32)
            acc[total * ROWS + i] = here

    def row_of(ref, c):
        return [ref[c, s] for s in range(HALF)]

    def own_pairs(c):
        combine(2, own, row_of(far, c), 0, c)
        combine(1, own, row_of(before, c), 0, c)

    def away_pairs(g, c):
        members = range(GROUPS[g][0], GROUPS[g][0] + GROUPS[g][1])
        combine(3, after[g], row_of(before, c), 1, c, members)
        combine(4, prior[g], row_of(far, c), 2, c, members)

    def complete(g):
        for c in range(GROUPS[g][0], GROUPS[g][0] + GROUPS[g][1]):
            pass_after(g, c).wait_recv()
            pass_before(g, c).wait_recv()
            keep_before(g, c).wait()

    last = ROWS - 1

    def arrivals(c):
        def on_after(g):
            to_previous(g, c).wait_recv()
            pass_after(g, c).start()

        per_group(c, on_after)
        for h in range(PIECES):
            to_next(c, h).wait_recv()

        def on_before(g):
            pass_before(g, c).start()
            keep_before(g, c).start()

        per_group(c, on_before)

    def spans(p, *entries):
        begin, end = 0, 0
        for when, low, high in entries:
            begin = jnp.where(when, low, begin)
            end = jnp.where(when, high, end)
        return begin, end

    @pl.loop(PIECES, ROWS * PIECES)
    def _(p):
        c = p // PIECES
        h = lax.rem(p, PIECES)
        relay_piece(c, h)

        @pl.when(h == 0)
        def _():
            arrivals(c - 1)

        @pl.when(p == 2 * PIECES)
        def _():
            @pl.loop(0, ROWS)
            def _(k):
                load(k).wait()
                to_partner(k).wait()

            spread.wait()

            @pl.when(jnp.logical_not(has_far))
            def _():
                fill.wait()

        def both(*tests):
            return functools.reduce(jnp.logical_and, tests)

        begin, end = spans(
            p,
            (both(h == 0, c >= 2), c - 1, c),
            (p == 11, 0, 1),
        )

        @pl.loop(begin, end)
        def _(k):
            own_pairs(k)

        begin, end = spans(p, (both(h == 1, c >= 2, c <= 5), 2 * c - 4, 2 * c - 2))

        @pl.loop(begin, end)
        def _(k):
            combine(0, own, [own[k * SLOTS + rep * HALF + s] for s in range(HALF)], 0, k)

        @pl.when(p == 14)
        def _():
            complete(0)

        begin, end = spans(
            p, (both(h == 2, c >= 4), c - 1, c), (p == 14, 0, 2), (p == 15, 2, 3)
        )

        @pl.loop(begin, end)
        def _(k):
            away_pairs(0, k)

        @pl.when(p == 25)
        def _():
            complete(1)

        begin, end = spans(
            p, (p == 25, 0, 2), (p == 26, 2, 4), (p == 27, 4, 6), (p == 30, 6, 7)
        )

        @pl.loop(begin, end)
        def _(k):
            away_pairs(1, k)

        @pl.when(p == 29)
        def _():
            complete(2)

        begin, end = spans(p, (p == 29, 0, 2), (p == 31, 2, 3))

        @pl.loop(begin, end)
        def _(k):
            away_pairs(2, 2 * k)
            away_pairs(2, 2 * k + 1)

    arrivals(last)
    away_pairs(0, last)
    away_pairs(1, last)
    away_pairs(2, last - 1)
    away_pairs(2, last)
    complete(3)

    @pl.loop(0, ROWS // 2)
    def _(k):
        away_pairs(3, 2 * k)
        away_pairs(3, 2 * k + 1)

    def sum_copy(slot, source, device):
        return remote(given.at[source], got.at[slot], sum_send.at[slot], sum_recv.at[slot], device)

    def add_up(t):
        given[t] = jnp.sum(acc[t * ROWS : t * ROWS + ROWS], axis=-1)

    up = [sum_copy(1, 1, (rep, at(1))), sum_copy(2, 1, (other, at(1)))]
    down = [sum_copy(3, 2, (rep, at(-1))), sum_copy(4, 2, (other, at(-1)))]
    across = sum_copy(0, 0, (other, row))
    add_up(1)
    add_up(2)

    @pl.when(jnp.logical_not(top))
    def _():
        for copy in up:
            copy.start()

    for copy in down:
        copy.start()
    own_pairs(last)
    add_up(0)
    across.start()

    @pl.when(row == 0)
    def _():
        got[1:3] = jnp.zeros((2, ROWS, TILE), jnp.float32)

    @pl.when(row > 0)
    def _():
        for copy in up:
            copy.wait_recv()

    for copy in down:
        copy.wait()
    across.wait()
    total = given[0]
    for slot in range(5):
        total += got[slot]
    out[...] = jnp.where(rep == 0, total[:, : TILE // 2], total[:, TILE // 2 :])

    for c in range(ROWS):
        for h in range(PIECES):
            @pl.when(gives_far)
            def _():
                to_far(c, h).wait_send()

            @pl.when(gives_next)
            def _():
                to_next(c, h).wait_send()

            @pl.when(relays)
            def _():
                relay(c, h).wait_send()

        g = group_of(c)
        to_previous(g, c).wait_send()
        pass_after(g, c).wait_send()
        pass_before(g, c).wait_send()

    @pl.when(jnp.logical_not(top))
    def _():
        for copy in up:
            copy.wait_send()


def body(blocks, tiles, tile_cols):
    dma = pltpu.SemaphoreType.DMA

    def stack(count):
        return pltpu.VMEM((count, TILE, TILE), jnp.bfloat16)

    half = pltpu.VMEM((ROWS, HALF, TILE, TILE), jnp.bfloat16)
    groups = [stack(count * SLOTS + 1) for _, count in GROUPS]
    pieces = ROWS * PIECES
    return pl.pallas_call(
        functools.partial(kernel, blocks),
        out_shape=jax.ShapeDtypeStruct((ROWS, TILE // 2), jnp.float32),
        in_specs=[
            pl.BlockSpec(memory_space=pltpu.HBM),
            pl.BlockSpec(memory_space=pltpu.HBM),
        ],
        out_specs=pl.BlockSpec(memory_space=pltpu.VMEM),
        scratch_shapes=[
            stack(NONE + 1),
            half,
            half,
            *groups,
            *groups,
            pltpu.VMEM((3 * ROWS, TILE, TILE), jnp.float32),
            pltpu.VMEM((3, ROWS, TILE), jnp.float32),
            pltpu.VMEM((5, ROWS, TILE), jnp.float32),
            pltpu.VMEM((SLOTS, blocks * ROWS), jnp.int32),
            pltpu.VMEM((3, HALF, TILE), jnp.int32),
            pltpu.VMEM((3, SLOTS, TILE), jnp.int32),
            pltpu.VMEM((len(PAIRS) * SLOTS, TILE), jnp.int32),
            pltpu.SMEM((len(PAIRS) * SLOTS, TILE), jnp.int32),
            dma((ROWS,)),
            dma((ROWS,)),
            dma,
            dma,
            dma,
            dma((ROWS,)),
            dma((ROWS,)),
            dma((pieces,)),
            dma((pieces,)),
            dma((pieces,)),
            dma((pieces,)),
            dma((ROWS,)),
            dma((ROWS,)),
            dma((ROWS,)),
            dma((ROWS,)),
            dma((ROWS,)),
            dma((ROWS,)),
            dma((5,)),
            dma((5,)),
            dma((pieces,)),
        ],
        compiler_params=pltpu.CompilerParams(
            collective_id=0, has_side_effects=True, vmem_limit_bytes=67_030_000
        ),
        name="triangles",
    )(tile_cols.T, tiles)


def solution(mesh):
    return jax.shard_map(
        functools.partial(body, mesh.shape["row"]),
        mesh=mesh,
        in_specs=(P("row", "rep", None, None), P()),
        out_specs=P("row", "rep"),
        check_vma=False,
    )
```

```python
import functools

import jax
import jax.numpy as jnp
from jax import lax
from jax.experimental import pallas as pl
from jax.experimental.pallas import tpu as pltpu
from jax.sharding import PartitionSpec as P

MESH = pl.DeviceIdType.MESH
TILE = 128
ROWS = 8
HALF = 8
SLOTS = 16
NONE = ROWS * SLOTS
DIST = 4
PIECES = 4
PIECE = HALF // PIECES
PAIRS = ((0, 0), (0, -1), (0, -DIST), (1, -1), (-1, -DIST))
GROUPS = ((0, 3), (3, 3), (6, 1), (7, 1))


def group_of(c):
    return next(g for g, (first, size) in enumerate(GROUPS) if first <= c < first + size)


def kernel(
    blocks,
    cols_hbm,
    tiles,
    out,
    own,
    before,
    far,
    after_0,
    after_1,
    after_2,
    after_3,
    prior_0,
    prior_1,
    prior_2,
    prior_3,
    acc,
    given,
    got,
    cols,
    of_k,
    of_i,
    found,
    table,
    local_sem,
    keep_sem,
    cols_sem,
    table_sem,
    fill_sem,
    pair_send,
    pair_recv,
    far_send,
    far_recv,
    before_send,
    before_recv,
    after_send,
    after_recv,
    pass_before_send,
    pass_before_recv,
    pass_after_send,
    pass_after_recv,
    sum_send,
    sum_recv,
    relay_send,
):
    after = (after_0, after_1, after_2, after_3)
    prior = (prior_0, prior_1, prior_2, prior_3)
    rep = lax.axis_index("rep")
    row = lax.axis_index("row")
    other = 1 - rep
    y = lax.rem(row, DIST)
    last_y = y == DIST - 1
    first_y = y == 0
    top = row == blocks - 1
    has_far = jnp.logical_or(row >= DIST - 1, row == 0)
    gives_far = jnp.logical_or(row <= blocks - DIST, top)
    gives_next = jnp.logical_not(last_y)

    def at(step):
        return lax.rem(row + step + blocks, blocks)

    barrier = pltpu.get_barrier_semaphore()

    def greet(device):
        pl.semaphore_signal(barrier, inc=1, device_id=device, device_id_type=MESH)

    greet((other, row))
    for step in (1, -1):
        greet((rep, at(step)))
        greet((other, at(step)))
    for step in (DIST, -DIST):
        greet((rep, at(step)))

    @pl.when(last_y)
    def _():
        greet((rep, at(1 - DIST)))

    @pl.when(first_y)
    def _():
        greet((rep, at(DIST - 1)))

    def remote(source, target, send, recv, device):
        return pltpu.make_async_remote_copy(
            source, target, send, recv, device_id=device, device_id_type=MESH
        )

    def load(c):
        return pltpu.make_async_copy(
            tiles.at[c], own.at[pl.ds(c * SLOTS + rep * HALF, HALF)], local_sem.at[c]
        )

    def to_partner(c):
        return remote(
            tiles.at[c], own.at[pl.ds(c * SLOTS + rep * HALF, HALF)],
            pair_send.at[c], pair_recv.at[c], (other, row),
        )

    def to_far(c, h):
        piece = pl.ds(h * PIECE, PIECE)
        place = c * PIECES + h
        return remote(
            tiles.at[c, piece], far.at[c, piece],
            far_send.at[place], far_recv.at[place], (rep, at(DIST)),
        )

    def to_next(c, h):
        piece = pl.ds(h * PIECE, PIECE)
        place = c * PIECES + h
        return remote(
            tiles.at[c, piece], before.at[c, piece],
            before_send.at[place], before_recv.at[place], (rep, at(1)),
        )

    def relay(c, h):
        piece = pl.ds(h * PIECE, PIECE)
        place = c * PIECES + h
        return remote(
            far.at[c, piece], before.at[c, piece],
            relay_send.at[place], before_recv.at[place], (rep, at(1 - DIST)),
        )

    def half_of(g, c):
        return pl.ds((c - GROUPS[g][0]) * SLOTS + rep * HALF, HALF)

    def to_previous(g, c):
        return remote(
            tiles.at[c], after[g].at[half_of(g, c)],
            after_send.at[c], after_recv.at[c], (rep, at(-1)),
        )

    def pass_after(g, c):
        return remote(
            after[g].at[half_of(g, c)], after[g].at[half_of(g, c)],
            pass_after_send.at[c], pass_after_recv.at[c], (other, row),
        )

    def pass_before(g, c):
        return remote(
            before.at[c], prior[g].at[half_of(g, c)],
            pass_before_send.at[c], pass_before_recv.at[c], (other, row),
        )

    def keep_before(g, c):
        return pltpu.make_async_copy(before.at[c], prior[g].at[half_of(g, c)], keep_sem.at[c])

    def per_group(c, action):
        for g, (first, size) in enumerate(GROUPS):

            @pl.when(jnp.logical_and(c >= first, c < first + size))
            def _():
                action(g)

    fetch = pltpu.make_async_copy(cols_hbm, cols, cols_sem)
    fetch.start()
    for c in range(ROWS):
        load(c).start()

    edge = jnp.logical_or(first_y, last_y).astype(jnp.int32)
    pl.semaphore_wait(barrier, 7 + edge)

    fill = pltpu.make_async_copy(tiles, far, fill_sem)

    @pl.when(jnp.logical_not(has_far))
    def _():
        fill.start()

    for c in range(ROWS):
        for h in range(PIECES):

            @pl.when(gives_far)
            def _():
                to_far(c, h).start()

            @pl.when(gives_next)
            def _():
                to_next(c, h).start()

        to_previous(group_of(c), c).start()
        to_partner(c).start()

    def relay_piece(c, h):
        @pl.when(has_far)
        def _():
            to_far(c, h).wait_recv()

        @pl.when(last_y)
        def _():
            relay(c, h).start()

    fetch.wait()
    known = cols[...].astype(jnp.float32)
    vertex = lax.broadcasted_iota(jnp.int32, (blocks * ROWS, TILE), 0)
    lane = lax.broadcasted_iota(jnp.int32, (blocks * ROWS, TILE), 1)

    def columns_at(wanted):
        pick = (vertex == wanted).astype(jnp.float32)
        return jnp.dot(
            known, pick, precision=lax.Precision.HIGHEST, preferred_element_type=jnp.float32
        ).astype(jnp.int32)

    for t, step in enumerate((0, -1, -DIST)):
        both = columns_at(at(step) * ROWS + lane % ROWS)
        of_k[t] = jnp.where(rep == 0, both[:HALF], both[HALF:])
    relay_piece(0, 0)
    for t, step in enumerate((0, 1, -1)):
        of_i[t] = columns_at(at(step) * ROWS + lane // ROWS)
    relay_piece(0, 1)
    lane = lax.broadcasted_iota(jnp.int32, (HALF, TILE), 1)
    index_i = lane // ROWS
    first = jnp.zeros_like(lane)
    size = jnp.ones_like(lane)
    for begin, count in GROUPS:
        inside = index_i >= begin
        first = jnp.where(inside, begin, first)
        size = jnp.where(inside, count, size)
    for pair, (step_i, step_k) in enumerate(PAIRS):
        if step_i == 0:
            base, none = index_i * SLOTS, jnp.full_like(lane, NONE)
        else:
            base, none = (index_i - first) * SLOTS, size * SLOTS
        own_col = at(step_k) * ROWS + lane % ROWS
        named = of_k[(0, -1, -DIST).index(step_k)]
        held = of_i[(0, 1, -1).index(step_i)]
        for part, wanted in enumerate((named, own_col)):
            place = none
            for s in range(SLOTS):
                same = jnp.logical_and(wanted == held[s : s + 1], wanted >= 0)
                place = jnp.where(same, base + s, place)
            found[pair * SLOTS + part * HALF : pair * SLOTS + part * HALF + HALF] = place
    relay_piece(0, 2)
    zero = jnp.zeros((TILE, TILE), jnp.bfloat16)
    own[NONE] = zero
    for g, (_, count) in enumerate(GROUPS):
        after[g][count * SLOTS] = zero
        prior[g][count * SLOTS] = zero
    acc[...] = jnp.zeros_like(acc)
    spread = pltpu.make_async_copy(found, table, table_sem)
    spread.start()
    relay_piece(0, 3)

    def combine(pair, rows_i, tiles_k, total, c, members=range(ROWS)):
        right = jnp.concatenate(tiles_k, axis=1)
        for i in members:
            column = i * ROWS + c
            left = rows_i[table[pair * SLOTS + HALF, column]]
            product = jnp.dot(left, right, preferred_element_type=jnp.float32)
            here = acc[total * ROWS + i]
            for s in range(HALF):
                weight = rows_i[table[pair * SLOTS + s, column]]
                here += product[:, s * TILE : s * TILE + TILE] * weight.astype(jnp.float32)
            acc[total * ROWS + i] = here

    def row_of(ref, c):
        return [ref[c, s] for s in range(HALF)]

    def own_pairs(c):
        combine(2, own, row_of(far, c), 0, c)
        combine(1, own, row_of(before, c), 0, c)

    def away_pairs(g, c):
        members = range(GROUPS[g][0], GROUPS[g][0] + GROUPS[g][1])
        combine(3, after[g], row_of(before, c), 1, c, members)
        combine(4, prior[g], row_of(far, c), 2, c, members)

    def complete(g):
        for c in range(GROUPS[g][0], GROUPS[g][0] + GROUPS[g][1]):
            pass_after(g, c).wait_recv()
            pass_before(g, c).wait_recv()
            keep_before(g, c).wait()

    last = ROWS - 1

    def arrivals(c):
        def on_after(g):
            to_previous(g, c).wait_recv()
            pass_after(g, c).start()

        per_group(c, on_after)
        for h in range(PIECES):
            to_next(c, h).wait_recv()

        def on_before(g):
            pass_before(g, c).start()
            keep_before(g, c).start()

        per_group(c, on_before)

    def spans(p, *entries):
        begin, end = 0, 0
        for when, low, high in entries:
            begin = jnp.where(when, low, begin)
            end = jnp.where(when, high, end)
        return begin, end

    @pl.loop(PIECES, ROWS * PIECES)
    def _(p):
        c = p // PIECES
        h = lax.rem(p, PIECES)
        relay_piece(c, h)

        @pl.when(h == 0)
        def _():
            arrivals(c - 1)

        @pl.when(p == 2 * PIECES)
        def _():
            @pl.loop(0, ROWS)
            def _(k):
                load(k).wait()
                to_partner(k).wait()

            spread.wait()

            @pl.when(jnp.logical_not(has_far))
            def _():
                fill.wait()

        def both(*tests):
            return functools.reduce(jnp.logical_and, tests)

        begin, end = spans(
            p,
            (both(h == 0, c >= 2), c - 1, c),
            (p == 11, 0, 1),
        )

        @pl.loop(begin, end)
        def _(k):
            own_pairs(k)

        begin, end = spans(p, (both(h == 1, c >= 2, c <= 5), 2 * c - 4, 2 * c - 2))

        @pl.loop(begin, end)
        def _(k):
            combine(0, own, [own[k * SLOTS + rep * HALF + s] for s in range(HALF)], 0, k)

        @pl.when(p == 14)
        def _():
            complete(0)

        begin, end = spans(
            p, (both(h == 2, c >= 4), c - 1, c), (p == 14, 0, 2), (p == 15, 2, 3)
        )

        @pl.loop(begin, end)
        def _(k):
            away_pairs(0, k)

        @pl.when(p == 25)
        def _():
            complete(1)

        begin, end = spans(
            p, (p == 25, 0, 2), (p == 26, 2, 4), (p == 27, 4, 6), (p == 30, 6, 7)
        )

        @pl.loop(begin, end)
        def _(k):
            away_pairs(1, k)

        @pl.when(p == 29)
        def _():
            complete(2)

        begin, end = spans(p, (p == 29, 0, 2), (p == 31, 2, 3))

        @pl.loop(begin, end)
        def _(k):
            away_pairs(2, 2 * k)
            away_pairs(2, 2 * k + 1)

    arrivals(last)
    away_pairs(0, last)
    away_pairs(1, last)
    away_pairs(2, last - 1)
    away_pairs(2, last)
    complete(3)

    @pl.loop(0, ROWS // 2)
    def _(k):
        away_pairs(3, 2 * k)
        away_pairs(3, 2 * k + 1)

    def sum_copy(slot, source, device):
        return remote(given.at[source], got.at[slot], sum_send.at[slot], sum_recv.at[slot], device)

    def add_up(t):
        given[t] = jnp.sum(acc[t * ROWS : t * ROWS + ROWS], axis=-1)

    up = [sum_copy(1, 1, (rep, at(1))), sum_copy(2, 1, (other, at(1)))]
    down = [sum_copy(3, 2, (rep, at(-1))), sum_copy(4, 2, (other, at(-1)))]
    across = sum_copy(0, 0, (other, row))
    add_up(1)
    add_up(2)

    @pl.when(jnp.logical_not(top))
    def _():
        for copy in up:
            copy.start()

    for copy in down:
        copy.start()
    own_pairs(last)
    add_up(0)
    across.start()

    @pl.when(row == 0)
    def _():
        got[1:3] = jnp.zeros((2, ROWS, TILE), jnp.float32)

    @pl.when(row > 0)
    def _():
        for copy in up:
            copy.wait_recv()

    for copy in down:
        copy.wait()
    across.wait()
    total = given[0]
    for slot in range(5):
        total += got[slot]
    out[...] = jnp.where(rep == 0, total[:, : TILE // 2], total[:, TILE // 2 :])

    for c in range(ROWS):
        for h in range(PIECES):
            @pl.when(gives_far)
            def _():
                to_far(c, h).wait_send()

            @pl.when(gives_next)
            def _():
                to_next(c, h).wait_send()

            @pl.when(last_y)
            def _():
                relay(c, h).wait_send()

        g = group_of(c)
        to_previous(g, c).wait_send()
        pass_after(g, c).wait_send()
        pass_before(g, c).wait_send()

    @pl.when(jnp.logical_not(top))
    def _():
        for copy in up:
            copy.wait_send()


def body(blocks, tiles, tile_cols):
    dma = pltpu.SemaphoreType.DMA

    def stack(count):
        return pltpu.VMEM((count, TILE, TILE), jnp.bfloat16)

    half = pltpu.VMEM((ROWS, HALF, TILE, TILE), jnp.bfloat16)
    groups = [stack(count * SLOTS + 1) for _, count in GROUPS]
    pieces = ROWS * PIECES
    return pl.pallas_call(
        functools.partial(kernel, blocks),
        out_shape=jax.ShapeDtypeStruct((ROWS, TILE // 2), jnp.float32),
        in_specs=[
            pl.BlockSpec(memory_space=pltpu.HBM),
            pl.BlockSpec(memory_space=pltpu.HBM),
        ],
        out_specs=pl.BlockSpec(memory_space=pltpu.VMEM),
        scratch_shapes=[
            stack(NONE + 1),
            half,
            half,
            *groups,
            *groups,
            pltpu.VMEM((3 * ROWS, TILE, TILE), jnp.float32),
            pltpu.VMEM((3, ROWS, TILE), jnp.float32),
            pltpu.VMEM((5, ROWS, TILE), jnp.float32),
            pltpu.VMEM((SLOTS, blocks * ROWS), jnp.int32),
            pltpu.VMEM((3, HALF, TILE), jnp.int32),
            pltpu.VMEM((3, SLOTS, TILE), jnp.int32),
            pltpu.VMEM((len(PAIRS) * SLOTS, TILE), jnp.int32),
            pltpu.SMEM((len(PAIRS) * SLOTS, TILE), jnp.int32),
            dma((ROWS,)),
            dma((ROWS,)),
            dma,
            dma,
            dma,
            dma((ROWS,)),
            dma((ROWS,)),
            dma((pieces,)),
            dma((pieces,)),
            dma((pieces,)),
            dma((pieces,)),
            dma((ROWS,)),
            dma((ROWS,)),
            dma((ROWS,)),
            dma((ROWS,)),
            dma((ROWS,)),
            dma((ROWS,)),
            dma((5,)),
            dma((5,)),
            dma((pieces,)),
        ],
        compiler_params=pltpu.CompilerParams(
            collective_id=0, has_side_effects=True, vmem_limit_bytes=67_030_000
        ),
        name="triangles",
    )(tile_cols.T, tiles)


def solution(mesh):
    return jax.shard_map(
        functools.partial(body, mesh.shape["row"]),
        mesh=mesh,
        in_specs=(P("row", "rep", None, None), P()),
        out_specs=P("row", "rep"),
        check_vma=False,
    )
```

```python
import functools

import jax
import jax.numpy as jnp
from jax import lax
from jax.experimental import pallas as pl
from jax.experimental.pallas import tpu as pltpu
from jax.sharding import PartitionSpec as P

MESH = pl.DeviceIdType.MESH
TILE = 128
ROWS = 8
HALF = 8
SLOTS = 16
NONE = ROWS * SLOTS
DIST = 4
PIECES = 4
PIECE = HALF // PIECES
PAIRS = ((0, 0), (0, -1), (0, -DIST), (1, -1), (-1, -DIST))
GROUPS = ((0, 3), (3, 3), (6, 1), (7, 1))


def group_of(c):
    return next(g for g, (first, size) in enumerate(GROUPS) if first <= c < first + size)


def kernel(
    blocks,
    cols_hbm,
    tiles,
    out,
    own,
    before,
    far,
    after_0,
    after_1,
    after_2,
    after_3,
    prior_0,
    prior_1,
    prior_2,
    prior_3,
    acc,
    given,
    got,
    cols,
    of_k,
    of_i,
    found,
    table,
    local_sem,
    keep_sem,
    cols_sem,
    table_sem,
    fill_sem,
    stand_sem,
    pair_send,
    pair_recv,
    far_send,
    far_recv,
    before_send,
    before_recv,
    after_send,
    after_recv,
    pass_before_send,
    pass_before_recv,
    pass_after_send,
    pass_after_recv,
    sum_send,
    sum_recv,
    relay_send,
):
    after = (after_0, after_1, after_2, after_3)
    prior = (prior_0, prior_1, prior_2, prior_3)
    rep = lax.axis_index("rep")
    row = lax.axis_index("row")
    other = 1 - rep
    y = lax.rem(row, DIST)
    last_y = y == DIST - 1
    first_y = y == 0
    top = row == blocks - 1
    has_far = jnp.logical_or(row >= DIST - 1, row == 0)
    gives_far = jnp.logical_or(row <= blocks - DIST, top)
    gives_next = jnp.logical_not(last_y)

    def at(step):
        return lax.rem(row + step + blocks, blocks)

    barrier = pltpu.get_barrier_semaphore()

    def greet(device):
        pl.semaphore_signal(barrier, inc=1, device_id=device, device_id_type=MESH)

    greet((other, row))
    greet((rep, at(-DIST)))

    @pl.when(row > 0)
    def _():
        greet((rep, at(-1)))

    @pl.when(jnp.logical_not(top))
    def _():
        greet((rep, at(1)))

    @pl.when(first_y)
    def _():
        greet((rep, at(DIST - 1)))

    def remote(source, target, send, recv, device):
        return pltpu.make_async_remote_copy(
            source, target, send, recv, device_id=device, device_id_type=MESH
        )

    def load(c):
        return pltpu.make_async_copy(
            tiles.at[c], own.at[pl.ds(c * SLOTS + rep * HALF, HALF)], local_sem.at[c]
        )

    def to_partner(c):
        return remote(
            tiles.at[c], own.at[pl.ds(c * SLOTS + rep * HALF, HALF)],
            pair_send.at[c], pair_recv.at[c], (other, row),
        )

    def to_far(c, h):
        piece = pl.ds(h * PIECE, PIECE)
        place = c * PIECES + h
        return remote(
            tiles.at[c, piece], far.at[c, piece],
            far_send.at[place], far_recv.at[place], (rep, at(DIST)),
        )

    def to_next(c, h):
        piece = pl.ds(h * PIECE, PIECE)
        place = c * PIECES + h
        return remote(
            tiles.at[c, piece], before.at[c, piece],
            before_send.at[place], before_recv.at[place], (rep, at(1)),
        )

    def relay(c, h):
        piece = pl.ds(h * PIECE, PIECE)
        place = c * PIECES + h
        return remote(
            far.at[c, piece], before.at[c, piece],
            relay_send.at[place], before_recv.at[place], (rep, at(1 - DIST)),
        )

    def half_of(g, c):
        return pl.ds((c - GROUPS[g][0]) * SLOTS + rep * HALF, HALF)

    def to_previous(g, c):
        return remote(
            tiles.at[c], after[g].at[half_of(g, c)],
            after_send.at[c], after_recv.at[c], (rep, at(-1)),
        )

    def pass_after(g, c):
        return remote(
            after[g].at[half_of(g, c)], after[g].at[half_of(g, c)],
            pass_after_send.at[c], pass_after_recv.at[c], (other, row),
        )

    def pass_before(g, c):
        return remote(
            before.at[c], prior[g].at[half_of(g, c)],
            pass_before_send.at[c], pass_before_recv.at[c], (other, row),
        )

    def keep_before(g, c):
        return pltpu.make_async_copy(before.at[c], prior[g].at[half_of(g, c)], keep_sem.at[c])

    def stand_in(g, c):
        return pltpu.make_async_copy(tiles.at[c], after[g].at[half_of(g, c)], stand_sem.at[c])

    def per_group(c, action):
        for g, (first, size) in enumerate(GROUPS):

            @pl.when(jnp.logical_and(c >= first, c < first + size))
            def _():
                action(g)

    fetch = pltpu.make_async_copy(cols_hbm, cols, cols_sem)
    fetch.start()
    for c in range(ROWS):
        load(c).start()

    ends = jnp.logical_or(row == 0, top).astype(jnp.int32)
    pl.semaphore_wait(barrier, 4 - ends + last_y.astype(jnp.int32))

    fill = pltpu.make_async_copy(tiles, far, fill_sem)

    @pl.when(jnp.logical_not(has_far))
    def _():
        fill.start()

    for c in range(ROWS):
        for h in range(PIECES):

            @pl.when(gives_far)
            def _():
                to_far(c, h).start()

            @pl.when(gives_next)
            def _():
                to_next(c, h).start()

        @pl.when(row > 0)
        def _():
            to_previous(group_of(c), c).start()

        @pl.when(top)
        def _():
            stand_in(group_of(c), c).start()

        to_partner(c).start()

    def relay_piece(c, h):
        @pl.when(has_far)
        def _():
            to_far(c, h).wait_recv()

        @pl.when(last_y)
        def _():
            relay(c, h).start()

    fetch.wait()
    known = cols[...].astype(jnp.float32)
    vertex = lax.broadcasted_iota(jnp.int32, (blocks * ROWS, TILE), 0)
    lane = lax.broadcasted_iota(jnp.int32, (blocks * ROWS, TILE), 1)

    def columns_at(wanted):
        pick = (vertex == wanted).astype(jnp.float32)
        return jnp.dot(
            known, pick, precision=lax.Precision.HIGHEST, preferred_element_type=jnp.float32
        ).astype(jnp.int32)

    for t, step in enumerate((0, -1, -DIST)):
        both = columns_at(at(step) * ROWS + lane % ROWS)
        of_k[t] = jnp.where(rep == 0, both[:HALF], both[HALF:])
    relay_piece(0, 0)
    for t, step in enumerate((0, 1, -1)):
        of_i[t] = columns_at(at(step) * ROWS + lane // ROWS)
    relay_piece(0, 1)
    lane = lax.broadcasted_iota(jnp.int32, (HALF, TILE), 1)
    index_i = lane // ROWS
    first = jnp.zeros_like(lane)
    size = jnp.ones_like(lane)
    for begin, count in GROUPS:
        inside = index_i >= begin
        first = jnp.where(inside, begin, first)
        size = jnp.where(inside, count, size)
    for pair, (step_i, step_k) in enumerate(PAIRS):
        if step_i == 0:
            base, none = index_i * SLOTS, jnp.full_like(lane, NONE)
        else:
            base, none = (index_i - first) * SLOTS, size * SLOTS
        own_col = at(step_k) * ROWS + lane % ROWS
        named = of_k[(0, -1, -DIST).index(step_k)]
        held = of_i[(0, 1, -1).index(step_i)]
        for part, wanted in enumerate((named, own_col)):
            place = none
            for s in range(SLOTS):
                same = jnp.logical_and(wanted == held[s : s + 1], wanted >= 0)
                place = jnp.where(same, base + s, place)
            found[pair * SLOTS + part * HALF : pair * SLOTS + part * HALF + HALF] = place
    relay_piece(0, 2)
    zero = jnp.zeros((TILE, TILE), jnp.bfloat16)
    own[NONE] = zero
    for g, (_, count) in enumerate(GROUPS):
        after[g][count * SLOTS] = zero
        prior[g][count * SLOTS] = zero
    acc[...] = jnp.zeros_like(acc)
    spread = pltpu.make_async_copy(found, table, table_sem)
    spread.start()
    relay_piece(0, 3)

    def combine(pair, rows_i, tiles_k, total, c, members=range(ROWS)):
        right = jnp.concatenate(tiles_k, axis=1)
        for i in members:
            column = i * ROWS + c
            left = rows_i[table[pair * SLOTS + HALF, column]]
            product = jnp.dot(left, right, preferred_element_type=jnp.float32)
            here = acc[total * ROWS + i]
            for s in range(HALF):
                weight = rows_i[table[pair * SLOTS + s, column]]
                here += product[:, s * TILE : s * TILE + TILE] * weight.astype(jnp.float32)
            acc[total * ROWS + i] = here

    def row_of(ref, c):
        return [ref[c, s] for s in range(HALF)]

    def own_pairs(c):
        combine(2, own, row_of(far, c), 0, c)
        combine(1, own, row_of(before, c), 0, c)

    def up_pair(g, c):
        combine(3, after[g], row_of(before, c), 1, c, rows_in(g))

    def down_pair(g, c):
        combine(4, prior[g], row_of(far, c), 2, c, rows_in(g))

    def away_pairs(g, c):
        up_pair(g, c)
        down_pair(g, c)

    def rows_in(g):
        return range(GROUPS[g][0], GROUPS[g][0] + GROUPS[g][1])

    def complete_after(g):
        for c in rows_in(g):
            pass_after(g, c).wait_recv()

    def complete_prior(g):
        for c in rows_in(g):
            pass_before(g, c).wait_recv()
            keep_before(g, c).wait()

    def complete(g):
        complete_after(g)
        complete_prior(g)

    last = ROWS - 1

    def after_arrives(c):
        def on_after(g):
            @pl.when(jnp.logical_not(top))
            def _():
                to_previous(g, c).wait_recv()

            @pl.when(top)
            def _():
                stand_in(g, c).wait()

            pass_after(g, c).start()

        per_group(c, on_after)

    def before_arrives(c):
        for h in range(PIECES):
            to_next(c, h).wait_recv()

        def on_before(g):
            pass_before(g, c).start()
            keep_before(g, c).start()

        per_group(c, on_before)

    def arrivals(c):
        after_arrives(c)
        before_arrives(c)

    def spans(p, *entries):
        begin, end = 0, 0
        for when, low, high in entries:
            begin = jnp.where(when, low, begin)
            end = jnp.where(when, high, end)
        return begin, end

    @pl.loop(PIECES, ROWS * PIECES)
    def _(p):
        c = p // PIECES
        h = lax.rem(p, PIECES)
        relay_piece(c, h)

        @pl.when(h == 0)
        def _():
            arrivals(c - 1)

        @pl.when(p == 2 * PIECES)
        def _():
            @pl.loop(0, ROWS)
            def _(k):
                load(k).wait()
                to_partner(k).wait()

            spread.wait()

            @pl.when(jnp.logical_not(has_far))
            def _():
                fill.wait()

        def both(*tests):
            return functools.reduce(jnp.logical_and, tests)

        begin, end = spans(
            p,
            (both(h == 0, c >= 2), c - 1, c),
            (p == 11, 0, 1),
        )

        @pl.loop(begin, end)
        def _(k):
            own_pairs(k)

        begin, end = spans(p, (both(h == 1, c >= 2, c <= 5), 2 * c - 4, 2 * c - 2))

        @pl.loop(begin, end)
        def _(k):
            combine(0, own, [own[k * SLOTS + rep * HALF + s] for s in range(HALF)], 0, k)

        @pl.when(p == 14)
        def _():
            complete(0)

        begin, end = spans(
            p, (both(h == 2, c >= 4), c - 1, c), (p == 14, 0, 2), (p == 15, 2, 3)
        )

        @pl.loop(begin, end)
        def _(k):
            away_pairs(0, k)

        @pl.when(p == 25)
        def _():
            complete(1)

        begin, end = spans(
            p, (p == 25, 0, 2), (p == 26, 2, 4), (p == 27, 4, 6), (p == 30, 6, 7)
        )

        @pl.loop(begin, end)
        def _(k):
            away_pairs(1, k)

        @pl.when(p == 29)
        def _():
            complete(2)

        begin, end = spans(p, (p == 29, 0, 2), (p == 31, 2, 3))

        @pl.loop(begin, end)
        def _(k):
            away_pairs(2, 2 * k)
            away_pairs(2, 2 * k + 1)

    after_arrives(last)
    away_pairs(2, last - 1)
    for g in range(3):
        down_pair(g, last)
    complete_after(3)

    @pl.loop(0, 3)
    def _(k):
        up_pair(3, 2 * k)
        up_pair(3, 2 * k + 1)

    up_pair(3, last - 1)
    combine(2, own, row_of(far, last), 0, last)
    before_arrives(last)
    for g in range(4):
        up_pair(g, last)

    def sum_copy(slot, source, device):
        return remote(given.at[source], got.at[slot], sum_send.at[slot], sum_recv.at[slot], device)

    def add_up(t):
        given[t] = jnp.sum(acc[t * ROWS : t * ROWS + ROWS], axis=-1)

    up = [sum_copy(1, 1, (rep, at(1))), sum_copy(2, 1, (other, at(1)))]
    down = [sum_copy(3, 2, (rep, at(-1))), sum_copy(4, 2, (other, at(-1)))]
    across = sum_copy(0, 0, (other, row))
    add_up(1)

    @pl.when(jnp.logical_not(top))
    def _():
        for copy in up:
            copy.start()

    combine(1, own, row_of(before, last), 0, last)
    complete_prior(3)

    @pl.loop(0, ROWS // 4)
    def _(k):
        for j in range(4):
            down_pair(3, 4 * k + j)

    add_up(2)
    for copy in down:
        copy.start()
    add_up(0)
    across.start()

    @pl.when(row == 0)
    def _():
        got[1:3] = jnp.zeros((2, ROWS, TILE), jnp.float32)

    @pl.when(row > 0)
    def _():
        for copy in up:
            copy.wait_recv()

    for copy in down:
        copy.wait()
    across.wait()
    total = given[0]
    for slot in range(5):
        total += got[slot]
    out[...] = jnp.where(rep == 0, total[:, : TILE // 2], total[:, TILE // 2 :])

    for c in range(ROWS):
        for h in range(PIECES):
            @pl.when(gives_far)
            def _():
                to_far(c, h).wait_send()

            @pl.when(gives_next)
            def _():
                to_next(c, h).wait_send()

            @pl.when(last_y)
            def _():
                relay(c, h).wait_send()

        g = group_of(c)

        @pl.when(row > 0)
        def _():
            to_previous(g, c).wait_send()

        pass_after(g, c).wait_send()
        pass_before(g, c).wait_send()

    @pl.when(jnp.logical_not(top))
    def _():
        for copy in up:
            copy.wait_send()


def body(blocks, tiles, tile_cols):
    dma = pltpu.SemaphoreType.DMA

    def stack(count):
        return pltpu.VMEM((count, TILE, TILE), jnp.bfloat16)

    half = pltpu.VMEM((ROWS, HALF, TILE, TILE), jnp.bfloat16)
    groups = [stack(count * SLOTS + 1) for _, count in GROUPS]
    pieces = ROWS * PIECES
    return pl.pallas_call(
        functools.partial(kernel, blocks),
        out_shape=jax.ShapeDtypeStruct((ROWS, TILE // 2), jnp.float32),
        in_specs=[
            pl.BlockSpec(memory_space=pltpu.HBM),
            pl.BlockSpec(memory_space=pltpu.HBM),
        ],
        out_specs=pl.BlockSpec(memory_space=pltpu.VMEM),
        scratch_shapes=[
            stack(NONE + 1),
            half,
            half,
            *groups,
            *groups,
            pltpu.VMEM((3 * ROWS, TILE, TILE), jnp.float32),
            pltpu.VMEM((3, ROWS, TILE), jnp.float32),
            pltpu.VMEM((5, ROWS, TILE), jnp.float32),
            pltpu.VMEM((SLOTS, blocks * ROWS), jnp.int32),
            pltpu.VMEM((3, HALF, TILE), jnp.int32),
            pltpu.VMEM((3, SLOTS, TILE), jnp.int32),
            pltpu.VMEM((len(PAIRS) * SLOTS, TILE), jnp.int32),
            pltpu.SMEM((len(PAIRS) * SLOTS, TILE), jnp.int32),
            dma((ROWS,)),
            dma((ROWS,)),
            dma,
            dma,
            dma,
            dma((ROWS,)),
            dma((ROWS,)),
            dma((ROWS,)),
            dma((pieces,)),
            dma((pieces,)),
            dma((pieces,)),
            dma((pieces,)),
            dma((ROWS,)),
            dma((ROWS,)),
            dma((ROWS,)),
            dma((ROWS,)),
            dma((ROWS,)),
            dma((ROWS,)),
            dma((5,)),
            dma((5,)),
            dma((pieces,)),
        ],
        compiler_params=pltpu.CompilerParams(
            collective_id=0, has_side_effects=True, vmem_limit_bytes=67_030_000
        ),
        name="triangles",
    )(tile_cols.T, tiles)


def solution(mesh):
    return jax.shard_map(
        functools.partial(body, mesh.shape["row"]),
        mesh=mesh,
        in_specs=(P("row", "rep", None, None), P()),
        out_specs=P("row", "rep"),
        check_vma=False,
    )
```

```python
import functools

import jax
import jax.numpy as jnp
from jax import lax
from jax.experimental import pallas as pl
from jax.experimental.pallas import tpu as pltpu
from jax.sharding import PartitionSpec as P

MESH = pl.DeviceIdType.MESH
TILE = 128
ROWS = 8
HALF = 8
SLOTS = 16
NONE = ROWS * SLOTS
DIST = 4
PIECES = 4
PIECE = HALF // PIECES
PAIRS = ((0, 0), (0, -1), (0, -DIST), (1, -1), (-1, -DIST))
GROUPS = ((0, 3), (3, 3), (6, 1), (7, 1))


def group_of(c):
    return next(g for g, (first, size) in enumerate(GROUPS) if first <= c < first + size)


def kernel(
    blocks,
    cols_hbm,
    tiles,
    out,
    own,
    before,
    far,
    after_0,
    after_1,
    after_2,
    after_3,
    prior_0,
    prior_1,
    prior_2,
    prior_3,
    acc,
    given,
    got,
    cols,
    of_k,
    of_i,
    found,
    table,
    local_sem,
    keep_sem,
    cols_sem,
    table_sem,
    fill_sem,
    stand_sem,
    pair_send,
    pair_recv,
    far_send,
    far_recv,
    before_send,
    before_recv,
    after_send,
    after_recv,
    pass_before_send,
    pass_before_recv,
    pass_after_send,
    pass_after_recv,
    sum_send,
    sum_recv,
    relay_send,
):
    after = (after_0, after_1, after_2, after_3)
    prior = (prior_0, prior_1, prior_2, prior_3)
    rep = lax.axis_index("rep")
    row = lax.axis_index("row")
    other = 1 - rep
    y = lax.rem(row, DIST)
    last_y = y == DIST - 1
    first_y = y == 0
    top = row == blocks - 1
    has_far = jnp.logical_or(row >= DIST - 1, row == 0)
    gives_far = jnp.logical_or(row <= blocks - DIST, top)
    gives_next = jnp.logical_not(last_y)

    def at(step):
        return lax.rem(row + step + blocks, blocks)

    barrier = pltpu.get_barrier_semaphore()

    def greet(device):
        pl.semaphore_signal(barrier, inc=1, device_id=device, device_id_type=MESH)

    greet((other, row))
    greet((rep, at(-DIST)))

    @pl.when(row > 0)
    def _():
        greet((rep, at(-1)))

    @pl.when(jnp.logical_not(top))
    def _():
        greet((rep, at(1)))

    @pl.when(first_y)
    def _():
        greet((rep, at(DIST - 1)))

    def remote(source, target, send, recv, device):
        return pltpu.make_async_remote_copy(
            source, target, send, recv, device_id=device, device_id_type=MESH
        )

    def load(c):
        return pltpu.make_async_copy(
            tiles.at[c], own.at[pl.ds(c * SLOTS + rep * HALF, HALF)], local_sem.at[c]
        )

    def to_partner(c):
        return remote(
            tiles.at[c], own.at[pl.ds(c * SLOTS + rep * HALF, HALF)],
            pair_send.at[c], pair_recv.at[c], (other, row),
        )

    def to_far(c, h):
        piece = pl.ds(h * PIECE, PIECE)
        place = c * PIECES + h
        return remote(
            tiles.at[c, piece], far.at[c, piece],
            far_send.at[place], far_recv.at[place], (rep, at(DIST)),
        )

    def to_next(c, h):
        piece = pl.ds(h * PIECE, PIECE)
        place = c * PIECES + h
        return remote(
            tiles.at[c, piece], before.at[c, piece],
            before_send.at[place], before_recv.at[place], (rep, at(1)),
        )

    def relay(c, h):
        piece = pl.ds(h * PIECE, PIECE)
        place = c * PIECES + h
        return remote(
            far.at[c, piece], before.at[c, piece],
            relay_send.at[place], before_recv.at[place], (rep, at(1 - DIST)),
        )

    def far_row(c):
        place = c * PIECES
        return remote(
            tiles.at[c], far.at[c], far_send.at[place], far_recv.at[place], (rep, at(DIST))
        )

    def next_row(c):
        place = c * PIECES
        return remote(
            tiles.at[c], before.at[c],
            before_send.at[place], before_recv.at[place], (rep, at(1)),
        )

    def half_of(g, c):
        return pl.ds((c - GROUPS[g][0]) * SLOTS + rep * HALF, HALF)

    def to_previous(g, c):
        return remote(
            tiles.at[c], after[g].at[half_of(g, c)],
            after_send.at[c], after_recv.at[c], (rep, at(-1)),
        )

    def pass_after(g, c):
        return remote(
            after[g].at[half_of(g, c)], after[g].at[half_of(g, c)],
            pass_after_send.at[c], pass_after_recv.at[c], (other, row),
        )

    def pass_before(g, c):
        return remote(
            before.at[c], prior[g].at[half_of(g, c)],
            pass_before_send.at[c], pass_before_recv.at[c], (other, row),
        )

    def keep_before(g, c):
        return pltpu.make_async_copy(before.at[c], prior[g].at[half_of(g, c)], keep_sem.at[c])

    def stand_in(g, c):
        return pltpu.make_async_copy(tiles.at[c], after[g].at[half_of(g, c)], stand_sem.at[c])

    def per_group(c, action):
        for g, (first, size) in enumerate(GROUPS):

            @pl.when(jnp.logical_and(c >= first, c < first + size))
            def _():
                action(g)

    fetch = pltpu.make_async_copy(cols_hbm, cols, cols_sem)
    fetch.start()
    for c in range(ROWS):
        load(c).start()

    ends = jnp.logical_or(row == 0, top).astype(jnp.int32)
    pl.semaphore_wait(barrier, 4 - ends + last_y.astype(jnp.int32))

    fill = pltpu.make_async_copy(tiles, far, fill_sem)

    @pl.when(jnp.logical_not(has_far))
    def _():
        fill.start()

    for c in range(ROWS):
        @pl.when(jnp.logical_and(gives_far, last_y))
        def _():
            for h in range(PIECES):
                to_far(c, h).start()

        @pl.when(jnp.logical_and(gives_far, jnp.logical_not(last_y)))
        def _():
            far_row(c).start()

        @pl.when(gives_next)
        def _():
            next_row(c).start()

        @pl.when(row > 0)
        def _():
            to_previous(group_of(c), c).start()

        @pl.when(top)
        def _():
            stand_in(group_of(c), c).start()

        to_partner(c).start()

    def relay_piece(c, h):
        @pl.when(last_y)
        def _():
            to_far(c, h).wait_recv()
            relay(c, h).start()

        @pl.when(
            functools.reduce(
                jnp.logical_and, (has_far, jnp.logical_not(last_y), h == PIECES - 1)
            )
        )
        def _():
            far_row(c).wait_recv()

    fetch.wait()
    known = cols[...].astype(jnp.float32)
    vertex = lax.broadcasted_iota(jnp.int32, (blocks * ROWS, TILE), 0)
    lane = lax.broadcasted_iota(jnp.int32, (blocks * ROWS, TILE), 1)

    def columns_at(wanted):
        pick = (vertex == wanted).astype(jnp.float32)
        return jnp.dot(
            known, pick, precision=lax.Precision.HIGHEST, preferred_element_type=jnp.float32
        ).astype(jnp.int32)

    for t, step in enumerate((0, -1, -DIST)):
        both = columns_at(at(step) * ROWS + lane % ROWS)
        of_k[t] = jnp.where(rep == 0, both[:HALF], both[HALF:])
    relay_piece(0, 0)
    for t, step in enumerate((0, 1, -1)):
        of_i[t] = columns_at(at(step) * ROWS + lane // ROWS)
    relay_piece(0, 1)
    lane = lax.broadcasted_iota(jnp.int32, (HALF, TILE), 1)
    index_i = lane // ROWS
    first = jnp.zeros_like(lane)
    size = jnp.ones_like(lane)
    for begin, count in GROUPS:
        inside = index_i >= begin
        first = jnp.where(inside, begin, first)
        size = jnp.where(inside, count, size)
    for pair, (step_i, step_k) in enumerate(PAIRS):
        if step_i == 0:
            base, none = index_i * SLOTS, jnp.full_like(lane, NONE)
        else:
            base, none = (index_i - first) * SLOTS, size * SLOTS
        own_col = at(step_k) * ROWS + lane % ROWS
        named = of_k[(0, -1, -DIST).index(step_k)]
        held = of_i[(0, 1, -1).index(step_i)]
        for part, wanted in enumerate((named, own_col)):
            place = none
            for s in range(SLOTS):
                same = jnp.logical_and(wanted == held[s : s + 1], wanted >= 0)
                place = jnp.where(same, base + s, place)
            found[pair * SLOTS + part * HALF : pair * SLOTS + part * HALF + HALF] = place
    relay_piece(0, 2)
    zero = jnp.zeros((TILE, TILE), jnp.bfloat16)
    own[NONE] = zero
    for g, (_, count) in enumerate(GROUPS):
        after[g][count * SLOTS] = zero
        prior[g][count * SLOTS] = zero
    acc[...] = jnp.zeros_like(acc)
    spread = pltpu.make_async_copy(found, table, table_sem)
    spread.start()
    relay_piece(0, 3)

    def combine(pair, rows_i, tiles_k, total, c, members=range(ROWS)):
        right = jnp.concatenate(tiles_k, axis=1)
        for i in members:
            column = i * ROWS + c
            left = rows_i[table[pair * SLOTS + HALF, column]]
            product = jnp.dot(left, right, preferred_element_type=jnp.float32)
            here = acc[total * ROWS + i]
            for s in range(HALF):
                weight = rows_i[table[pair * SLOTS + s, column]]
                here += product[:, s * TILE : s * TILE + TILE] * weight.astype(jnp.float32)
            acc[total * ROWS + i] = here

    def row_of(ref, c):
        return [ref[c, s] for s in range(HALF)]

    def own_pairs(c):
        combine(2, own, row_of(far, c), 0, c)
        combine(1, own, row_of(before, c), 0, c)

    def up_pair(g, c):
        combine(3, after[g], row_of(before, c), 1, c, rows_in(g))

    def down_pair(g, c):
        combine(4, prior[g], row_of(far, c), 2, c, rows_in(g))

    def away_pairs(g, c):
        up_pair(g, c)
        down_pair(g, c)

    def rows_in(g):
        return range(GROUPS[g][0], GROUPS[g][0] + GROUPS[g][1])

    def complete_after(g):
        for c in rows_in(g):
            pass_after(g, c).wait_recv()

    def complete_prior(g):
        for c in rows_in(g):
            pass_before(g, c).wait_recv()
            keep_before(g, c).wait()

    def complete(g):
        complete_after(g)
        complete_prior(g)

    last = ROWS - 1

    def after_arrives(c):
        def on_after(g):
            @pl.when(jnp.logical_not(top))
            def _():
                to_previous(g, c).wait_recv()

            @pl.when(top)
            def _():
                stand_in(g, c).wait()

            pass_after(g, c).start()

        per_group(c, on_after)

    def before_arrives(c):
        @pl.when(first_y)
        def _():
            for h in range(PIECES):
                to_next(c, h).wait_recv()

        @pl.when(jnp.logical_not(first_y))
        def _():
            next_row(c).wait_recv()

        def on_before(g):
            pass_before(g, c).start()
            keep_before(g, c).start()

        per_group(c, on_before)

    def arrivals(c):
        after_arrives(c)
        before_arrives(c)

    def spans(p, *entries):
        begin, end = 0, 0
        for when, low, high in entries:
            begin = jnp.where(when, low, begin)
            end = jnp.where(when, high, end)
        return begin, end

    @pl.loop(PIECES, ROWS * PIECES)
    def _(p):
        c = p // PIECES
        h = lax.rem(p, PIECES)
        relay_piece(c, h)

        @pl.when(h == 0)
        def _():
            arrivals(c - 1)

        @pl.when(p == 2 * PIECES)
        def _():
            @pl.loop(0, ROWS)
            def _(k):
                load(k).wait()
                to_partner(k).wait()

            spread.wait()

            @pl.when(jnp.logical_not(has_far))
            def _():
                fill.wait()

        def both(*tests):
            return functools.reduce(jnp.logical_and, tests)

        begin, end = spans(
            p,
            (both(h == 0, c >= 2), c - 1, c),
            (p == 11, 0, 1),
        )

        @pl.loop(begin, end)
        def _(k):
            own_pairs(k)

        begin, end = spans(p, (both(h == 1, c >= 2, c <= 5), 2 * c - 4, 2 * c - 2))

        @pl.loop(begin, end)
        def _(k):
            combine(0, own, [own[k * SLOTS + rep * HALF + s] for s in range(HALF)], 0, k)

        @pl.when(p == 14)
        def _():
            complete(0)

        begin, end = spans(
            p, (both(h == 2, c >= 4), c - 1, c), (p == 14, 0, 2), (p == 15, 2, 3)
        )

        @pl.loop(begin, end)
        def _(k):
            away_pairs(0, k)

        @pl.when(p == 25)
        def _():
            complete(1)

        begin, end = spans(
            p, (p == 25, 0, 2), (p == 26, 2, 4), (p == 27, 4, 6), (p == 30, 6, 7)
        )

        @pl.loop(begin, end)
        def _(k):
            away_pairs(1, k)

        @pl.when(p == 29)
        def _():
            complete(2)

        begin, end = spans(p, (p == 29, 0, 2), (p == 31, 2, 3))

        @pl.loop(begin, end)
        def _(k):
            away_pairs(2, 2 * k)
            away_pairs(2, 2 * k + 1)

    after_arrives(last)
    away_pairs(2, last - 1)
    for g in range(3):
        down_pair(g, last)
    complete_after(3)

    @pl.loop(0, 3)
    def _(k):
        up_pair(3, 2 * k)
        up_pair(3, 2 * k + 1)

    up_pair(3, last - 1)
    combine(2, own, row_of(far, last), 0, last)

    def sum_copy(slot, source, device):
        return remote(given.at[source], got.at[slot], sum_send.at[slot], sum_recv.at[slot], device)

    def add_up(t):
        given[t] = jnp.sum(acc[t * ROWS : t * ROWS + ROWS], axis=-1)

    up = [sum_copy(1, 1, (rep, at(1))), sum_copy(2, 1, (other, at(1)))]
    down = [sum_copy(3, 2, (rep, at(-1))), sum_copy(4, 2, (other, at(-1)))]
    across = sum_copy(0, 0, (other, row))
    @pl.when(row == 0)
    def _():
        add_up(0)
        add_up(1)
        for copy in (across, *up):
            copy.start()

    before_arrives(last)

    @pl.when(row > 0)
    def _():
        for g in range(4):
            up_pair(g, last)

    @pl.when(row > 0)
    def _():
        add_up(1)

    @pl.when(jnp.logical_and(row > 0, jnp.logical_not(top)))
    def _():
        for copy in up:
            copy.start()

    complete_prior(3)

    for k in range(ROWS):
        down_pair(3, k)

    add_up(2)
    for copy in down:
        copy.start()

    @pl.when(row > 0)
    def _():
        combine(1, own, row_of(before, last), 0, last)

    @pl.when(row > 0)
    def _():
        add_up(0)
        across.start()

    @pl.when(row == 0)
    def _():
        got[1:3] = jnp.zeros((2, ROWS, TILE), jnp.float32)

    @pl.when(row > 0)
    def _():
        for copy in up:
            copy.wait_recv()

    for copy in down:
        copy.wait()
    across.wait()
    total = given[0]
    for slot in range(5):
        total += got[slot]
    out[...] = jnp.where(rep == 0, total[:, : TILE // 2], total[:, TILE // 2 :])

    for c in range(ROWS):
        @pl.when(jnp.logical_and(gives_far, last_y))
        def _():
            for h in range(PIECES):
                to_far(c, h).wait_send()

        @pl.when(jnp.logical_and(gives_far, jnp.logical_not(last_y)))
        def _():
            far_row(c).wait_send()

        @pl.when(gives_next)
        def _():
            next_row(c).wait_send()

        @pl.when(last_y)
        def _():
            for h in range(PIECES):
                relay(c, h).wait_send()

        g = group_of(c)

        @pl.when(row > 0)
        def _():
            to_previous(g, c).wait_send()

        pass_after(g, c).wait_send()
        pass_before(g, c).wait_send()

    @pl.when(jnp.logical_not(top))
    def _():
        for copy in up:
            copy.wait_send()


def body(blocks, tiles, tile_cols):
    dma = pltpu.SemaphoreType.DMA

    def stack(count):
        return pltpu.VMEM((count, TILE, TILE), jnp.bfloat16)

    half = pltpu.VMEM((ROWS, HALF, TILE, TILE), jnp.bfloat16)
    groups = [stack(count * SLOTS + 1) for _, count in GROUPS]
    pieces = ROWS * PIECES
    return pl.pallas_call(
        functools.partial(kernel, blocks),
        out_shape=jax.ShapeDtypeStruct((ROWS, TILE // 2), jnp.float32),
        in_specs=[
            pl.BlockSpec(memory_space=pltpu.HBM),
            pl.BlockSpec(memory_space=pltpu.HBM),
        ],
        out_specs=pl.BlockSpec(memory_space=pltpu.VMEM),
        scratch_shapes=[
            stack(NONE + 1),
            half,
            half,
            *groups,
            *groups,
            pltpu.VMEM((3 * ROWS, TILE, TILE), jnp.float32),
            pltpu.VMEM((3, ROWS, TILE), jnp.float32),
            pltpu.VMEM((5, ROWS, TILE), jnp.float32),
            pltpu.VMEM((SLOTS, blocks * ROWS), jnp.int32),
            pltpu.VMEM((3, HALF, TILE), jnp.int32),
            pltpu.VMEM((3, SLOTS, TILE), jnp.int32),
            pltpu.VMEM((len(PAIRS) * SLOTS, TILE), jnp.int32),
            pltpu.SMEM((len(PAIRS) * SLOTS, TILE), jnp.int32),
            dma((ROWS,)),
            dma((ROWS,)),
            dma,
            dma,
            dma,
            dma((ROWS,)),
            dma((ROWS,)),
            dma((ROWS,)),
            dma((pieces,)),
            dma((pieces,)),
            dma((pieces,)),
            dma((pieces,)),
            dma((ROWS,)),
            dma((ROWS,)),
            dma((ROWS,)),
            dma((ROWS,)),
            dma((ROWS,)),
            dma((ROWS,)),
            dma((5,)),
            dma((5,)),
            dma((pieces,)),
        ],
        compiler_params=pltpu.CompilerParams(
            collective_id=0, has_side_effects=True, vmem_limit_bytes=67_030_000
        ),
        name="triangles",
    )(tile_cols.T, tiles)


def solution(mesh):
    return jax.shard_map(
        functools.partial(body, mesh.shape["row"]),
        mesh=mesh,
        in_specs=(P("row", "rep", None, None), P()),
        out_specs=P("row", "rep"),
        check_vma=False,
    )
```
